32 devices in a mesh: group: 4 (over y, x), brick: 8 (over z, core).
Axes of the slice: x: 2, y: 2, z: 4, core: 2. Of those that a mesh axis runs over, the one named last changes fastest.
Arguments:
- populations: float32 [19, 8, 64, 128], P(None, 'group', 'brick'), may hold values from 0 to 1, as said below
- positions: float32 [3, 64, 642], P(None, ('group', 'brick')), may hold values from -6 to 6
- rest_shape: float32 [3, 642], replicated, may hold values from -6 to 6
- inverse: float32 [642, 642], replicated, may hold values from -2 to 2, as said below
- sample_cells: int32 [32, 64], P(('group', 'brick')), may hold values from 0 to 2047
- vertex_slots: int32 [32, 1284], P(('group', 'brick')), may hold values from 0 to 63, as said below
- pair_own: int32 [32, 2048], P(('group', 'brick')), may hold values from 0 to 1283
- pair_far: int32 [32, 2048], P(('group', 'brick')), may hold values from 0 to 1283
Outputs:
- new_populations: float32 [19, 8, 64, 128], P(None, 'group', 'brick')
- new_positions: float32 [3, 64, 642], P(None, ('group', 'brick'))
The draws below stay inside these ranges and needn't reach their ends.
Inputs may be any that keep to these rules, and one draw needn't show every extreme that they name: Every population is positive and a cell's populations sum to between 0.6 and 1.4. inverse is symmetric. `vertex_slots`: on every device each slot 0 to 63 is named by at least one vertex.
All inputs are finite; a program needn't handle non-finite values.
Results may differ from the reference program's by a relative error of at most 0.0001.
Values sent between devices are 32-bit elements; how exact they have to be, the bound alone decides.
A program may use at most 64 MiB of HBM per device.

```python
import jax
import jax.numpy as jnp
from jax import lax

V = 642
B_DEV = 2
CX = 2
CY = 8
NZ = 128
C_PEER = 8
NPAIR = 2048
ITERS = 4
STEPS = 2
NX = 8
NY = 64
SLOTS = 64
BODIES = 64
N_GROUP = 4
N_BRICK = 8


weights_table = [1.0 / 3.0] + [1.0 / 18.0] * 6 + [1.0 / 36.0] * 12


def draw_populations(key, part):
    weight_col = jnp.array(weights_table, jnp.float32)[:, None, None, None]
    dims = (19, NX, NY, NZ)
    factor = 1.0 + jnp.clip(0.15 * jax.random.normal(key, dims, jnp.float32), -0.4, 0.4)
    return weight_col * factor


def draw_inverse(key, part):
    noise = jax.random.normal(key, (V, V), jnp.float32)
    noise = noise / jnp.sqrt(jnp.float32(V))
    symmetric = (noise + noise.T) * 0.7071
    return 0.5 * (jnp.eye(V, dtype=jnp.float32) + 0.25 * symmetric)


def draw_vertex_slots(key, part):
    keys = jax.random.split(jax.random.fold_in(key, 7), N_GROUP * N_BRICK)
    orders = jax.vmap(lambda single: jax.random.permutation(single, B_DEV * V))(keys)
    return (orders % (C_PEER * N_BRICK)).astype(jnp.int32)


def place_ends(drawn, stream_key, smallest, top_value):
    index_at = [jax.random.randint(jax.random.fold_in(stream_key, axis), (), 0, length) for axis, length in enumerate(drawn.shape)]
    longest = drawn.shape.index(max(drawn.shape))
    beside = index_at[:longest] + [(index_at[longest] + 1) % drawn.shape[longest]] + index_at[longest + 1:]
    return drawn.at[tuple(index_at)].set(smallest).at[tuple(beside)].set(top_value)


def block_levels(key, shape, pieces, least, largest):
    level = 1.0
    for axis_at, blocks in pieces:
        steps = jax.random.uniform(jax.random.fold_in(jax.random.fold_in(key, 6), axis_at), (blocks,), jnp.float32, least / len(pieces), largest / len(pieces))
        level = level * jnp.repeat(jnp.exp(steps), shape[axis_at] // blocks).reshape((-1,) + (1,) * (len(shape) - 1 - axis_at))
    return level


def bell_draw(key, extent, width, reach, shards=(), kind=jnp.bfloat16):
    factor_of = block_levels(key, extent, shards, -0.22, 0.18) if shards else 1.0
    drawn = jax.random.normal(key, extent, jnp.float32) * width * factor_of
    return jnp.minimum(jnp.maximum(drawn, -reach), reach).astype(kind)


def setup_inputs(seed: int = 0) -> dict:
    splits = jax.random.split(jax.random.key(seed), 9)
    return {
        "populations": draw_populations(jax.random.fold_in(splits[8], 71), 0),
        "positions": bell_draw(splits[1], (3, BODIES, V), 1.0, 6.0, ((1, 32),), jnp.float32),
        "rest_shape": bell_draw(splits[2], (3, V), 1.0, 6.0, (), jnp.float32),
        "inverse": draw_inverse(jax.random.fold_in(splits[8], 71), 0),
        "sample_cells": place_ends(jax.random.randint(splits[4], (N_GROUP * N_BRICK, SLOTS), 0, CX * CY * NZ), jax.random.fold_in(splits[4], 1), 0, (CX * CY * NZ) - 1).astype(jnp.int32),
        "vertex_slots": draw_vertex_slots(jax.random.fold_in(splits[8], 71), 0),
        "pair_own": place_ends(jax.random.randint(splits[6], (N_GROUP * N_BRICK, NPAIR), 0, B_DEV * V), jax.random.fold_in(splits[6], 1), 0, (B_DEV * V) - 1).astype(jnp.int32),
        "pair_far": place_ends(jax.random.randint(splits[7], (N_GROUP * N_BRICK, NPAIR), 0, B_DEV * V), jax.random.fold_in(splits[7], 1), 0, (B_DEV * V) - 1).astype(jnp.int32),
    }


velocities = [(0, 0, 0), (0, 0, 1), (0, 0, -1), (1, 0, 0), (-1, 0, 0), (0, 1, 0), (0, -1, 0),
              (1, 1, 0), (-1, -1, 0), (1, -1, 0), (-1, 1, 0), (1, 0, 1), (-1, 0, -1), (1, 0, -1),
              (-1, 0, 1), (0, 1, 1), (0, -1, -1), (0, 1, -1), (0, -1, 1)]
weights_table = [1.0 / 3.0] + [1.0 / 18.0] * 6 + [1.0 / 36.0] * 12
relax_time = 0.8
contact_gain = 0.5
contact_range = 6.0
coupling_gain = 0.05
mass_weight = 1.0
shape_weight = 1.0
time_step = 1.0


def moments(populations):
    table = jnp.array(velocities, jnp.float32)
    density = jnp.sum(populations, axis=0)
    momentum = jnp.einsum("iq,ixyz->qxyz", table, populations, precision=lax.Precision.HIGHEST)
    return density, momentum


def collide(populations, force):
    table = jnp.array(velocities, jnp.float32)
    weight_col = jnp.array(weights_table, jnp.float32)[:, None, None, None]
    density, momentum = moments(populations)
    veloc = (momentum + 0.5 * force) / density
    project = jnp.einsum("iq,qxyz->ixyz", table, veloc, precision=lax.Precision.HIGHEST)
    forcing = jnp.einsum("iq,qxyz->ixyz", table, force, precision=lax.Precision.HIGHEST)
    square = jnp.sum(veloc * veloc, axis=0)
    equil = weight_col * density * (1.0 + 3.0 * project + 4.5 * project * project - 1.5 * square)
    return populations - (populations - equil) / relax_time + 3.0 * weight_col * forcing


def stream(post):
    moved = [jnp.roll(post[index], velocities[index], axis=(0, 1, 2)) for index in range(19)]
    return jnp.stack(moved, axis=0)


def to_blocks(field):
    parts = field.reshape(3, N_GROUP, CX, N_BRICK, CY, NZ).transpose(0, 1, 3, 2, 4, 5)
    return parts.reshape(3, N_GROUP, N_BRICK, CX * CY * NZ)


def from_blocks(blocks):
    parts = blocks.reshape(3, N_GROUP, N_BRICK, CX, CY, NZ).transpose(0, 1, 3, 2, 4, 5)
    return parts.reshape(3, N_GROUP * CX, N_BRICK * CY, NZ)


def add_rows(values, index, count):
    return jnp.zeros((3, count), jnp.float32).at[:, index].add(values)


def reference(populations, positions, rest_shape, inverse, sample_cells, vertex_slots, pair_own, pair_far):
    devices = N_GROUP * N_BRICK
    cells = CX * CY * NZ
    verts = B_DEV * V
    slot_count = C_PEER * N_BRICK
    dist = populations
    shape = positions.reshape(3, devices, verts)
    request = sample_cells.reshape(N_GROUP, N_BRICK, slot_count)
    for step_index in range(STEPS):
        density, momentum = moments(dist)
        flow = momentum / density
        picked = jnp.take_along_axis(to_blocks(flow), request[None], axis=3)
        received = picked.reshape(3, N_GROUP, N_BRICK, N_BRICK, C_PEER).transpose(0, 1, 3, 2, 4)
        received = received.reshape(3, devices, slot_count)
        vertex_flow = jnp.take_along_axis(received, vertex_slots[None], axis=2)
        predicted = shape + time_step * vertex_flow
        for sweep_index in range(ITERS):
            lower = jnp.roll(shape.reshape(3, N_GROUP, N_BRICK, verts), 1, axis=2).reshape(3, devices, verts)
            own_points = jnp.take_along_axis(shape, pair_own[None], axis=2)
            far_points = jnp.take_along_axis(lower, pair_far[None], axis=2)
            diff = own_points - far_points
            weight = jnp.exp(-jnp.sum(diff * diff, axis=0) / contact_range)
            push = contact_gain * weight * diff
            contact = jax.vmap(lambda values, index: add_rows(values, index, verts), in_axes=(1, 0), out_axes=1)(push, pair_own)
            bodies = shape.reshape(3, devices, B_DEV, V)
            centroid = jnp.mean(bodies, axis=3, keepdims=True)
            target = (centroid + rest_shape[:, None, None, :]).reshape(3, devices, verts)
            rhs = mass_weight * predicted + shape_weight * target + contact
            shape = jnp.dot(rhs.reshape(3 * devices * B_DEV, V), inverse,
                            precision=lax.Precision.HIGHEST, preferred_element_type=jnp.float32).reshape(3, devices, verts)
        vertex_force = coupling_gain * (shape - predicted)
        slot_force = jax.vmap(lambda values, index: add_rows(values, index, slot_count), in_axes=(1, 0), out_axes=1)(vertex_force, vertex_slots)
        back = slot_force.reshape(3, N_GROUP, N_BRICK, N_BRICK, C_PEER).transpose(0, 1, 3, 2, 4)
        back = back.reshape(3, devices, slot_count)
        cell_force = jax.vmap(lambda values, index: add_rows(values, index, cells), in_axes=(1, 0), out_axes=1)(back, sample_cells)
        force = from_blocks(cell_force.reshape(3, N_GROUP, N_BRICK, cells))
        dist = stream(collide(dist, force))
    return dist, shape.reshape(3, devices * B_DEV, V)
```

```python
import functools

import jax
import jax.numpy as jnp
from jax import lax
from jax.experimental import pallas as pl
from jax.experimental.pallas import tpu as pltpu
from jax.sharding import PartitionSpec as P

ITERS = 4
STEPS = 2

velocities = [
    (0, 0, 0),
    (0, 0, 1),
    (0, 0, -1),
    (1, 0, 0),
    (-1, 0, 0),
    (0, 1, 0),
    (0, -1, 0),
    (1, 1, 0),
    (-1, -1, 0),
    (1, -1, 0),
    (-1, 1, 0),
    (1, 0, 1),
    (-1, 0, -1),
    (1, 0, -1),
    (-1, 0, 1),
    (0, 1, 1),
    (0, -1, -1),
    (0, 1, -1),
    (0, -1, 1),
]
weights_table = [1.0 / 3.0] + [1.0 / 18.0] * 6 + [1.0 / 36.0] * 12
DIRS = len(velocities)
relax_time = 0.8
contact_gain = 0.5
contact_range = 6.0
coupling_gain = 0.05
mass_weight = 1.0
shape_weight = 1.0
time_step = 1.0

LANES = 128
BODY_ROWS = 4
GROUP = 32
RING = 2
MESH = pl.DeviceIdType.MESH


def up(value, unit):
    return -(-value // unit) * unit


def take(rows, index):
    return jnp.take_along_axis(rows, index, axis=1, mode="promise_in_bounds")


def halves(value):
    high = value.astype(jnp.bfloat16).astype(jnp.float32)
    return high, value - high


def signed_sum(terms, axis):
    total = None
    for p in range(1, DIRS, 2):
        sign = velocities[p][axis]
        if sign == 0:
            continue
        if total is None:
            assert sign > 0
            total = terms[p]
        else:
            total = total + terms[p] if sign > 0 else total - terms[p]
    return total


def moments(rows):
    density = functools.reduce(lambda a, b: a + b, rows)
    opposite = {p: rows[p] - rows[p + 1] for p in range(1, DIRS, 2)}
    return density, [signed_sum(opposite, axis) for axis in range(3)]


def dot_c(vector, p):
    total = None
    for axis in range(3):
        sign = velocities[p][axis]
        if sign == 0:
            continue
        if total is None:
            total = vector[axis] if sign > 0 else -vector[axis]
        else:
            total = total + vector[axis] if sign > 0 else total - vector[axis]
    return total


def collide(rows, force):
    density, momentum = moments(rows)
    inverse_density = 1.0 / density
    veloc = [(momentum[a] + 0.5 * force[a]) * inverse_density for a in range(3)]
    square = veloc[0] * veloc[0] + veloc[1] * veloc[1] + veloc[2] * veloc[2]
    keep, gain = 1.0 - 1.0 / relax_time, 1.0 / relax_time
    base = 1.0 - 1.5 * square
    scaled = [density * (gain * w) for w in (1.0 / 3.0, 1.0 / 18.0, 1.0 / 36.0)]
    out = [None] * DIRS
    out[0] = keep * rows[0] + scaled[0] * base
    for p in range(1, DIRS, 2):
        weight = weights_table[p]
        rho = scaled[1] if p < 7 else scaled[2]
        along = dot_c(veloc, p)
        even = rho * (base + 4.5 * (along * along))
        odd = rho * (3.0 * along) + (3.0 * weight) * dot_c(force, p)
        out[p] = keep * rows[p] + (even + odd)
        out[p + 1] = keep * rows[p + 1] + (even - odd)
    return out


def roll_z(value, index):
    step = velocities[index][2]
    if step == 0:
        return value
    return pltpu.roll(value, step % LANES, 1)


def step_kernel(
    sizes, pop_ref, pos_ref, rest_in, inv_hbm, cells_ref, slots_ref, own_ref, far_ref,
    outf_ref, outp_ref,
    inv_raw, inv_tail, inv_high, inv_mid, hot, mask, lhs, spread, slot_hot, deposit, row_id, turned,
    shapes, lower, rest8, slot8, slot_flat, cells_own, cells_near,
    flow_out, flow_in, force_out, force_in, blocks, edges_out, edges_in, fluid, post, fluid_2, post_2,
    field, field_2,
    inv_sem, ring_send, ring_recv, flow_send, flow_recv, force_send, force_recv,
    cells_send, cells_recv, edge_send, edge_recv, block_send, block_recv,
):
    n_brick, n_group, verts, bodies, slot_count = sizes
    me = lax.axis_index("brick")
    group = lax.axis_index("group")
    cx, cy = pop_ref.shape[1:3]
    width = shapes.shape[2]
    blocks_v = width // LANES
    rows_v = bodies * BODY_ROWS
    tiles = own_ref.shape[0]
    peer_cells = slot_count // n_brick
    wide = n_brick * GROUP
    wide_tiles = wide // LANES
    slot_tiles = cells_own.shape[1] // LANES
    long_y = cy + 2 * RING
    short_y = cy + 2
    part = cx * long_y
    f32, bf16, i32 = jnp.float32, jnp.bfloat16, jnp.int32

    def brick_at(offset):
        return lax.rem(me + (offset + n_brick), n_brick)

    def group_at(offset):
        return lax.rem(group + (offset + n_group), n_group)

    def iota(shape, axis):
        return lax.broadcasted_iota(i32, shape, axis)

    near = [(dg, o) for dg in (0, 1, -1) for o in range(n_brick) if (dg, o) != (0, 0)]
    barrier = pltpu.get_barrier_semaphore()
    for dg, o in near:
        pl.semaphore_signal(barrier, inc=1, device_id=(group_at(dg), brick_at(o)), device_id_type=MESH)
    inv_copy = pltpu.make_async_copy(inv_hbm, inv_raw, inv_sem)
    inv_copy.start()

    def remote(source, target, send, recv, dg, o):
        copy = pltpu.make_async_remote_copy(
            src_ref=source, dst_ref=target, send_sem=send, recv_sem=recv,
            device_id=(group_at(dg), brick_at(o)), device_id_type=MESH,
        )
        copy.start()
        return copy

    def all_bytes(ref, sem):
        pltpu.make_async_copy(ref, ref, sem).wait()

    shapes[0] = jnp.zeros((rows_v, width), f32)
    rest8[...] = jnp.zeros((rows_v, width), f32)
    for b in range(bodies):
        for c in range(3):
            r = b * BODY_ROWS + c
            shapes[0, r : r + 1, 0:verts] = pos_ref[c, b : b + 1, :]
            rest8[r : r + 1, 0:verts] = rest_in[c : c + 1, :]
    cells_own[...] = jnp.zeros(cells_own.shape, i32)
    cells_own[:, 0:slot_count] = cells_ref[...]
    for x in range(cx):
        for i in range(DIRS):
            edges_out[0, i, 2 * x : 2 * x + 2, :] = pop_ref[i, x, 0:RING, :]
            edges_out[1, i, 2 * x : 2 * x + 2, :] = pop_ref[i, x, cy - RING : cy, :]

    lane8 = iota((8, LANES), 1)
    sub8 = iota((8, LANES), 0)
    in_group = lane8 % GROUP
    of_group = lane8 // GROUP

    def sample(flow, step):
        lines = cx * cy
        got = []
        for t in range(slot_tiles):
            cell = cells_own[0:1, t * LANES : (t + 1) * LANES]
            at = jnp.broadcast_to(cell & (LANES - 1), (lines, LANES))
            chosen = jnp.broadcast_to(cell >> 7, (lines, LANES)) == iota((lines, LANES), 0)
            got.append([
                jnp.sum(jnp.where(chosen, take(flow[c], at), 0.0), axis=0, keepdims=True) for c in range(3)
            ])
        for base in range(0, n_brick, 8):
            start = base * peer_cells
            t, offset = start // LANES, start % LANES
            index = (offset + sub8 * peer_cells + in_group) & (LANES - 1)
            message = jnp.zeros((8, LANES), f32)
            for c in range(3):
                moved = take(jnp.broadcast_to(got[t][c], (8, LANES)), index)
                message = jnp.where(of_group == c, moved, message)
            for s in range(8):
                flow_out[step, base + s] = message[s : s + 1, :]

    def send_flow(step):
        pltpu.make_async_copy(flow_out.at[step, me], flow_in.at[step, me], flow_recv.at[step]).start()
        for o in range(1, n_brick):
            remote(
                flow_out.at[step, brick_at(o)], flow_in.at[step, me],
                flow_send.at[step], flow_recv.at[step], 0, o,
            )

    def send_ring(k):
        return remote(shapes.at[k], lower.at[k], ring_send.at[k], ring_recv.at[k], 0, 1)

    lines_own = [
        jnp.concatenate([pop_ref[i, x] for x in range(cx)], axis=0) for i in range(DIRS)
    ]
    density, momentum = moments(lines_own)
    inverse_density = 1.0 / density
    sample([m * inverse_density for m in momentum], 0)

    pl.semaphore_wait(barrier, len(near))
    send_flow(0)
    copies = [send_ring(0)]
    for n, (dg, db) in enumerate([(a, b) for a in (-1, 0, 1) for b in (-1, 0, 1) if (a, b) != (0, 0)]):
        copies.append(remote(
            cells_own, cells_near.at[1 - dg, 1 - db], cells_send.at[n], cells_recv.at[n], dg, db
        ))
    cells_copies = copies[1:]
    edge_copies = [
        remote(
            edges_out.at[side], edges_in.at[1 - dg, side],
            edge_send.at[dg + 1, side], edge_recv.at[dg + 1, side], dg, 1 if side else -1,
        )
        for dg in (0, -1, 1)
        for side in (0, 1)
    ]
    block_copies = [
        remote(pop_ref, blocks.at[n], block_send.at[n], block_recv.at[n], dg, 0)
        for n, dg in enumerate((1, -1))
    ]

    def place(index):
        body = jnp.zeros(index.shape, i32)
        for b in range(1, bodies):
            body = body + jnp.where(index >= b * verts, 1, 0)
        vertex = index - body * verts
        return vertex & (LANES - 1), vertex >> 7, body

    own_lane, own_block, own_body = place(own_ref[...])
    far_lane, far_block, far_body = place(far_ref[...])
    own_id = own_body * blocks_v + own_block
    far_id = far_body * blocks_v + far_block

    lane_square = iota((LANES, LANES), 1)
    turned[0:tiles, :] = own_lane.astype(f32)
    turned[tiles:LANES, :] = jnp.zeros((LANES - tiles, LANES), f32)
    columns = jnp.transpose(turned[...]).astype(i32)
    for t in range(tiles):
        column = jnp.broadcast_to(columns[:, t : t + 1], (LANES, LANES))
        hot[t * LANES : (t + 1) * LANES, :] = jnp.where(column == lane_square, 1.0, 0.0).astype(bf16)
        chosen = jnp.broadcast_to(own_block[t : t + 1, :], (blocks_v * rows_v, LANES))
        mask[t] = jnp.where(
            chosen == iota((blocks_v * rows_v, LANES), 0) // rows_v, 1.0, 0.0
        ).astype(bf16)
    spread[...] = jnp.zeros(spread.shape, f32)

    slot_flat[...] = jnp.zeros(slot_flat.shape, i32)
    slot_flat[:, 0 : bodies * verts] = slots_ref[...]
    flat = jnp.broadcast_to(slot_flat[...], (8, slot_flat.shape[1]))
    total = slot_flat.shape[1]
    picked = flat[:, :width]
    row_body = iota((rows_v, width), 0) // BODY_ROWS
    for b in range(1, bodies):
        moved = pltpu.roll(flat, total - b * verts, 1)[:, :width]
        picked = jnp.where(row_body == b, moved, picked)
    slot8[...] = jnp.where(iota((rows_v, width), 1) < verts, picked, -1)

    inv_copy.wait()
    chunk = 32
    full = verts // chunk
    edge = verts // LANES * LANES
    for ref in (inv_high, inv_mid):
        ref[:, edge:width] = jnp.zeros((width, width - edge), bf16)
        ref[full * chunk : width, :] = jnp.zeros((width - full * chunk, width), bf16)

    def split(n, _):
        at = pl.multiple_of(n * chunk, chunk)
        high, mid = halves(inv_raw[pl.ds(at, chunk), :])
        inv_high[pl.ds(at, chunk), 0:verts] = high.astype(bf16)
        inv_mid[pl.ds(at, chunk), 0:verts] = mid.astype(bf16)
        return 0

    lax.fori_loop(0, full, split, 0)
    if verts % chunk:
        inv_tail[...] = jnp.zeros(inv_tail.shape, f32)
        inv_tail[0 : verts % chunk, 0:verts] = inv_raw[full * chunk : verts, :]
        high, mid = halves(inv_tail[...])
        inv_high[full * chunk : (full + 1) * chunk, :] = high.astype(bf16)
        inv_mid[full * chunk : (full + 1) * chunk, :] = mid.astype(bf16)

    def pick(ref, k, lane, ident):
        total = [jnp.zeros((tiles, LANES), f32)] * 3
        for b in range(bodies):
            for h in range(blocks_v):
                chosen = ident == b * blocks_v + h
                for c in range(3):
                    r = b * BODY_ROWS + c
                    row = ref[k, r : r + 1, h * LANES : (h + 1) * LANES]
                    got = take(jnp.broadcast_to(row, (tiles, LANES)), lane)
                    total[c] = jnp.where(chosen, got, total[c])
        return total

    def contact(k, while_waiting):
        own = pick(shapes, k, own_lane, own_id)
        while_waiting()
        copies_ring[k].wait_recv()
        far = pick(lower, k, far_lane, far_id)
        diff = [a - b for a, b in zip(own, far)]
        square = diff[0] * diff[0] + diff[1] * diff[1] + diff[2] * diff[2]
        scale = contact_gain * jnp.exp(-square / contact_range)
        for b in range(bodies):
            for c in range(3):
                r = b * BODY_ROWS + c
                spread[r * tiles : (r + 1) * tiles, :] = jnp.where(own_body == b, scale * diff[c], 0.0)
        half = blocks_v * rows_v
        for t in range(tiles):
            push = spread[pl.ds(t, rows_v, stride=tiles), :]
            for n, piece in enumerate(halves(push)):
                pair = jnp.concatenate([piece, piece], axis=0).astype(bf16)
                lhs[n * half : (n + 1) * half, t * LANES : (t + 1) * LANES] = (
                    jnp.concatenate([pair] * (blocks_v // 2), axis=0) * mask[t]
                )
        added = jnp.dot(lhs[...], hot[...], preferred_element_type=f32)
        added = added[:half] + added[half:]
        return jnp.concatenate([added[h * rows_v : (h + 1) * rows_v] for h in range(blocks_v)], axis=1)

    copies_ring = {0: copies[0]}

    def received(step):
        all_bytes(flow_in.at[step], flow_recv.at[step])
        out = []
        per_tile = LANES // peer_cells
        for t in range(slot_tiles):
            index = (sub8 % BODY_ROWS) * GROUP + lane8 % peer_cells
            table = jnp.zeros((8, LANES), f32)
            for s in range(t * per_tile, min((t + 1) * per_tile, n_brick)):
                moved = take(jnp.broadcast_to(flow_in[step, s], (8, LANES)), index)
                table = jnp.where(lane8 // peer_cells == s % per_tile, moved, table)
            out.append(table)
        return out

    def vertex_flow(step):
        tables = received(step)
        parts = []
        for h in range(blocks_v):
            slot = jnp.maximum(slot8[:, h * LANES : (h + 1) * LANES], 0)
            got = take(tables[0], slot & (LANES - 1))
            for t in range(1, slot_tiles):
                got = jnp.where(slot >> 7 == t, take(tables[t], slot & (LANES - 1)), got)
            parts.append(got)
        return jnp.concatenate(parts, axis=1)

    def relax(predicted, touch, k):
        shape = shapes[k - 1]
        centroid = jnp.sum(shape, axis=1, keepdims=True) * (1.0 / verts)
        rhs = mass_weight * predicted + shape_weight * (centroid + rest8[...]) + touch
        left = jnp.concatenate(halves(rhs), axis=0).astype(bf16)
        both = jnp.dot(left, inv_high[...], preferred_element_type=f32) + jnp.dot(
            left, inv_mid[...], preferred_element_type=f32
        )
        shapes[k] = both[:rows_v] + both[rows_v:]

    def build_slots():
        column_of = []
        for h in range(blocks_v):
            rows = slot8[:, h * LANES : (h + 1) * LANES].astype(f32)
            turned[h * rows_v : (h + 1) * rows_v, :] = rows
        columns = jnp.transpose(turned[...]).astype(i32)
        for t in range(wide_tiles):
            q = iota((LANES, LANES), 1)
            brick = q // GROUP + t * (LANES // GROUP)
            inner = q % GROUP
            target = brick - 1 + inner // peer_cells
            target = jnp.where(target < 0, target + n_brick, target)
            target = jnp.where(target >= n_brick, target - n_brick, target)
            slot = jnp.where(inner < 3 * peer_cells, target * peer_cells + inner % peer_cells, -2)
            for b in range(bodies):
                for h in range(blocks_v):
                    at = h * rows_v + b * BODY_ROWS
                    column = jnp.broadcast_to(columns[:, at : at + 1], (LANES, LANES))
                    slot_hot[b, h * LANES : (h + 1) * LANES, t * LANES : (t + 1) * LANES] = jnp.where(
                        column == slot, 1.0, 0.0
                    ).astype(bf16)

    def build_deposit():
        for copy in cells_copies:
            copy.wait_recv()
        per_tile = LANES // GROUP
        for dg in range(3):
            for t in range(wide_tiles):
                start = t * per_tile * peer_cells
                source, offset = start // LANES, start % LANES
                index = offset + of_group * peer_cells + in_group % peer_cells
                side = in_group // peer_cells
                cell = jnp.zeros((8, LANES), i32)
                for db in range(3):
                    ref = cells_own if (dg, db) == (1, 1) else cells_near.at[dg, db]
                    row = ref[0:1, source * LANES : (source + 1) * LANES]
                    moved = take(jnp.broadcast_to(row, (8, LANES)), index)
                    cell = jnp.where(side == db, moved, cell)
                line = cell >> 7
                x = jnp.zeros((8, LANES), i32)
                for edge_x in range(1, cx):
                    x = x + jnp.where(line >= edge_x * cy, 1, 0)
                y = line - x * cy + cy * (side - 1) + RING
                inside = (y >= 0) & (y < long_y) & (side < 3)
                at = dg * wide_tiles + t
                row_id[dg, :, t * LANES : (t + 1) * LANES] = jnp.where(inside, x * long_y + y, -1)
                turned[at : at + 1, :] = (cell & (LANES - 1))[0:1, :].astype(f32)
        columns = jnp.transpose(turned[...]).astype(i32)
        for dg in range(3):
            for t in range(wide_tiles):
                at = dg * wide_tiles + t
                column = jnp.broadcast_to(columns[:, at : at + 1], (LANES, LANES))
                deposit[dg, t * LANES : (t + 1) * LANES, :] = jnp.where(
                    column == lane_square, 1.0, 0.0
                ).astype(bf16)

    def build_fluid():
        for copy in edge_copies + block_copies:
            copy.wait_recv()
        for i in range(DIRS):
            for dg in range(3):
                source = pop_ref if dg == 1 else blocks.at[0 if dg == 0 else 1]
                for x in range(cx):
                    at = (dg * cx + x) * long_y
                    fluid[i, at + RING : at + RING + cy, :] = source[i, x]
                    fluid[i, at + RING + cy : at + long_y, :] = edges_in[dg, 0, i, 2 * x : 2 * x + 2, :]
                    fluid[i, at : at + RING, :] = edges_in[dg, 1, i, 2 * x : 2 * x + 2, :]

    def send_force(predicted, k, step):
        change = coupling_gain * (shapes[k] - predicted)
        left = jnp.concatenate(halves(change), axis=0).astype(bf16)
        total = None
        for b in range(bodies):
            got = jnp.dot(left, slot_hot[b], preferred_element_type=f32)
            got = got[:rows_v] + got[rows_v:]
            if b:
                got = pltpu.roll(got, rows_v - b * BODY_ROWS, 0)
            total = got if total is None else total + got
        per_tile = LANES // GROUP
        index = (sub8 % per_tile) * GROUP + in_group
        for base in range(0, n_brick, 8):
            message = jnp.zeros((8, LANES), f32)
            for c in range(3):
                for n in range(8 // per_tile):
                    t = base // per_tile + n
                    row = total[c : c + 1, t * LANES : (t + 1) * LANES]
                    moved = take(jnp.broadcast_to(row, (8, LANES)), index)
                    chosen = (of_group == c) & (sub8 // per_tile == n)
                    message = jnp.where(chosen, moved, message)
            for s in range(8):
                force_out[step, base + s] = message[s : s + 1, :]
        pltpu.make_async_copy(
            force_out.at[step, me], force_in.at[step, n_brick + me], force_recv.at[step]
        ).start()
        for dg, o in near:
            remote(
                force_out.at[step, brick_at(o)], force_in.at[step, (1 - dg) * n_brick + me],
                force_send.at[step], force_recv.at[step], dg, o,
            )

    def gather_force(step):
        all_bytes(force_in.at[step], force_recv.at[step])
        per_tile = LANES // GROUP
        index = jnp.minimum(sub8, 3) * GROUP + in_group
        for dg in range(3):
            parts = []
            for t in range(wide_tiles):
                table = jnp.zeros((8, LANES), f32)
                for n in range(per_tile):
                    row = force_in[step, dg * n_brick + t * per_tile + n]
                    moved = take(jnp.broadcast_to(row, (8, LANES)), index)
                    table = jnp.where(of_group == n, moved, table)
                parts.append(table)
            table = jnp.concatenate(parts, axis=1)
            ids = jnp.broadcast_to(row_id[dg, 0:1, :], (part, wide))
            chosen = ids == iota((part, wide), 0)
            left = []
            pieces = halves(table)
            for c in range(3):
                for piece in pieces:
                    row = jnp.broadcast_to(piece[c : c + 1, :], (part, wide))
                    left.append(jnp.where(chosen, row, 0.0))
            left = jnp.concatenate(left, axis=0).astype(bf16)
            got = jnp.dot(left, deposit[dg], preferred_element_type=f32)
            for c in range(3):
                field[c, dg * part : (dg + 1) * part, :] = (
                    got[2 * c * part : (2 * c + 1) * part] + got[(2 * c + 1) * part : (2 * c + 2) * part]
                )

    def nothing():
        pass

    background = {0: nothing, 1: build_slots, 2: build_deposit, 3: build_fluid}
    k = 0
    for step in range(STEPS):
        touch = contact(k, background.get(k, nothing))
        predicted = shapes[k] + time_step * vertex_flow(step)
        for sweep in range(ITERS):
            k += 1
            relax(predicted, touch, k)
            if sweep < ITERS - 1:
                copies_ring[k] = send_ring(k)
                touch = contact(k, background.get(k, nothing))
        send_force(predicted, k, step)
        if step < STEPS - 1:
            copies_ring[k] = send_ring(k)
            gather_force(step)
            for q in range(3 * part // 8):
                rows = slice(8 * q, 8 * q + 8)
                after = collide([fluid[i, rows, :] for i in range(DIRS)], [field[c, rows, :] for c in range(3)])
                for i in range(DIRS):
                    post[i, rows, :] = roll_z(after[i], i)
            for i in range(DIRS):
                step_x, step_y, _ = velocities[i]
                for x in range(cx + 2):
                    at = (x + 1 - step_x) * long_y + 1 - step_y
                    fluid_2[i, x * short_y : (x + 1) * short_y, :] = post[i, at : at + short_y, :]
            lines_own = [
                jnp.concatenate(
                    [fluid_2[i, (x + 1) * short_y + 1 : (x + 1) * short_y + 1 + cy, :] for x in range(cx)], axis=0
                )
                for i in range(DIRS)
            ]
            density, momentum = moments(lines_own)
            inverse_density = 1.0 / density
            sample([m * inverse_density for m in momentum], step + 1)
            send_flow(step + 1)

    for b in range(bodies):
        for c in range(3):
            r = b * BODY_ROWS + c
            outp_ref[c, b : b + 1, :] = shapes[k, r : r + 1, 0:verts]
    gather_force(STEPS - 1)
    for c in range(3):
        for x in range(cx + 2):
            at = (x + 1) * long_y + 1
            field_2[c, x * short_y : (x + 1) * short_y, :] = field[c, at : at + short_y, :]
    for q in range((cx + 2) * short_y // 8):
        rows = slice(8 * q, 8 * q + 8)
        after = collide([fluid_2[i, rows, :] for i in range(DIRS)], [field_2[c, rows, :] for c in range(3)])
        for i in range(DIRS):
            post_2[i, rows, :] = roll_z(after[i], i)
    for i in range(DIRS):
        step_x, step_y, _ = velocities[i]
        for x in range(cx):
            at = (x + 1 - step_x) * short_y + 1 - step_y
            outf_ref[i, x] = post_2[i, at : at + cy, :]

    for copy in copies_ring.values():
        copy.wait_send()
    for copy in cells_copies + edge_copies + block_copies:
        copy.wait_send()
    for step in range(STEPS):
        all_bytes(flow_out.at[step, pl.ds(0, n_brick - 1)], flow_send.at[step])
        all_bytes(force_in.at[step, pl.ds(0, 3 * n_brick - 1)], force_send.at[step])


def on_device(
    populations, positions, rest_shape, inverse, sample_cells, vertex_slots, pair_own, pair_far
):
    n_brick = lax.axis_size("brick")
    n_group = lax.axis_size("group")
    slot_count = sample_cells.shape[1]
    bodies, verts = positions.shape[1:]
    width = up(verts, LANES)
    rows = bodies * BODY_ROWS
    dirs, cx, cy, lanes = populations.shape
    tiles = pair_own.shape[1] // LANES
    wide = n_brick * GROUP
    long_rows = 3 * cx * (cy + 2 * RING)
    short_rows = (cx + 2) * (cy + 2)
    sweeps = STEPS * ITERS
    blocks_v = width // LANES
    f32, bf16, i32 = jnp.float32, jnp.bfloat16, jnp.int32
    vmem = pltpu.VMEM
    dma = pltpu.SemaphoreType.DMA
    in_vmem = pl.BlockSpec(memory_space=pltpu.VMEM)
    return pl.pallas_call(
        functools.partial(step_kernel, (n_brick, n_group, verts, bodies, slot_count)),
        out_shape=(
            jax.ShapeDtypeStruct(populations.shape, f32),
            jax.ShapeDtypeStruct(positions.shape, f32),
        ),
        in_specs=[in_vmem, in_vmem, in_vmem, pl.BlockSpec(memory_space=pl.ANY)] + [in_vmem] * 4,
        out_specs=(in_vmem, in_vmem),
        scratch_shapes=[
            vmem((verts, verts), f32),
            vmem((32, width), f32),
            vmem((width, width), bf16),
            vmem((width, width), bf16),
            vmem((tiles * LANES, LANES), bf16),
            vmem((tiles, blocks_v * rows, LANES), bf16),
            vmem((2 * blocks_v * rows, tiles * LANES), bf16),
            vmem((rows * tiles, LANES), f32),
            vmem((bodies, width, wide), bf16),
            vmem((3, wide, LANES), bf16),
            vmem((3, 8, wide), i32),
            vmem((LANES, LANES), f32),
            vmem((sweeps + 1, rows, width), f32),
            vmem((sweeps, rows, width), f32),
            vmem((rows, width), f32),
            vmem((rows, width), i32),
            vmem((1, up(bodies * verts + width, LANES)), i32),
            vmem((1, up(slot_count, LANES)), i32),
            vmem((3, 3, 1, up(slot_count, LANES)), i32),
            vmem((STEPS, n_brick, 1, LANES), f32),
            vmem((STEPS, n_brick, 1, LANES), f32),
            vmem((STEPS, n_brick, 1, LANES), f32),
            vmem((STEPS, 3 * n_brick, 1, LANES), f32),
            vmem((2,) + populations.shape, f32),
            vmem((2, dirs, 2 * cx, LANES), f32),
            vmem((3, 2, dirs, 2 * cx, LANES), f32),
            vmem((dirs, long_rows, LANES), f32),
            vmem((dirs, long_rows, LANES), f32),
            vmem((dirs, short_rows, LANES), f32),
            vmem((dirs, short_rows, LANES), f32),
            vmem((3, long_rows, LANES), f32),
            vmem((3, short_rows, LANES), f32),
            dma,
            dma((sweeps,)),
            dma((sweeps,)),
            dma((STEPS,)),
            dma((STEPS,)),
            dma((STEPS,)),
            dma((STEPS,)),
            dma((8,)),
            dma((8,)),
            dma((3, 2)),
            dma((3, 2)),
            dma((2,)),
            dma((2,)),
        ],
        compiler_params=pltpu.CompilerParams(
            collective_id=0, has_side_effects=True, vmem_limit_bytes=60 * 1024 * 1024
        ),
    )(
        populations, positions, rest_shape, inverse, sample_cells, vertex_slots,
        pair_own.reshape(tiles, LANES), pair_far.reshape(tiles, LANES),
    )


def solution(mesh):
    placed = (
        P(None, "group", "brick", None),
        P(None, ("group", "brick"), None),
        P(),
        P(),
        P(("group", "brick"), None),
        P(("group", "brick"), None),
        P(("group", "brick"), None),
        P(("group", "brick"), None),
    )
    return jax.shard_map(
        on_device,
        mesh=mesh,
        in_specs=placed,
        out_specs=(P(None, "group", "brick", None), P(None, ("group", "brick"), None)),
        check_vma=False,
    )
```

```python
import functools

import jax
import jax.numpy as jnp
from jax import lax
from jax.experimental import pallas as pl
from jax.experimental.pallas import tpu as pltpu
from jax.sharding import PartitionSpec as P

ITERS = 4
STEPS = 2

velocities = [
    (0, 0, 0),
    (0, 0, 1),
    (0, 0, -1),
    (1, 0, 0),
    (-1, 0, 0),
    (0, 1, 0),
    (0, -1, 0),
    (1, 1, 0),
    (-1, -1, 0),
    (1, -1, 0),
    (-1, 1, 0),
    (1, 0, 1),
    (-1, 0, -1),
    (1, 0, -1),
    (-1, 0, 1),
    (0, 1, 1),
    (0, -1, -1),
    (0, 1, -1),
    (0, -1, 1),
]
weights_table = [1.0 / 3.0] + [1.0 / 18.0] * 6 + [1.0 / 36.0] * 12
DIRS = len(velocities)
relax_time = 0.8
contact_gain = 0.5
contact_range = 6.0
coupling_gain = 0.05
mass_weight = 1.0
shape_weight = 1.0
time_step = 1.0

LANES = 128
BODY_ROWS = 4
GROUP = 32
RING = 2
MESH = pl.DeviceIdType.MESH


def up(value, unit):
    return -(-value // unit) * unit


def take(rows, index):
    return jnp.take_along_axis(rows, index, axis=1, mode="promise_in_bounds")


def halves(value):
    high = value.astype(jnp.bfloat16).astype(jnp.float32)
    return high, value - high


def signed_sum(terms, axis):
    total = None
    for p in range(1, DIRS, 2):
        sign = velocities[p][axis]
        if sign == 0:
            continue
        if total is None:
            assert sign > 0
            total = terms[p]
        else:
            total = total + terms[p] if sign > 0 else total - terms[p]
    return total


def moments(rows):
    density = functools.reduce(lambda a, b: a + b, rows)
    opposite = {p: rows[p] - rows[p + 1] for p in range(1, DIRS, 2)}
    return density, [signed_sum(opposite, axis) for axis in range(3)]


def dot_c(vector, p):
    total = None
    for axis in range(3):
        sign = velocities[p][axis]
        if sign == 0:
            continue
        if total is None:
            total = vector[axis] if sign > 0 else -vector[axis]
        else:
            total = total + vector[axis] if sign > 0 else total - vector[axis]
    return total


def collide(rows, force):
    density, momentum = moments(rows)
    inverse_density = 1.0 / density
    veloc = [(momentum[a] + 0.5 * force[a]) * inverse_density for a in range(3)]
    square = veloc[0] * veloc[0] + veloc[1] * veloc[1] + veloc[2] * veloc[2]
    keep, gain = 1.0 - 1.0 / relax_time, 1.0 / relax_time
    base = 1.0 - 1.5 * square
    scaled = [density * (gain * w) for w in (1.0 / 3.0, 1.0 / 18.0, 1.0 / 36.0)]
    out = [None] * DIRS
    out[0] = keep * rows[0] + scaled[0] * base
    for p in range(1, DIRS, 2):
        weight = weights_table[p]
        rho = scaled[1] if p < 7 else scaled[2]
        along = dot_c(veloc, p)
        even = rho * (base + 4.5 * (along * along))
        odd = rho * (3.0 * along) + (3.0 * weight) * dot_c(force, p)
        out[p] = keep * rows[p] + (even + odd)
        out[p + 1] = keep * rows[p + 1] + (even - odd)
    return out


def roll_z(value, index):
    step = velocities[index][2]
    if step == 0:
        return value
    return pltpu.roll(value, step % LANES, 1)


def step_kernel(
    sizes, pop_hbm, pos_hbm, rest_hbm, inv_hbm, cells_hbm, slots_hbm, own_hbm, far_hbm,
    outf_ref, outp_ref,
    pop_ref, pos_ref, rest_in, cells_ref, slots_ref, pairs,
    inv_raw, inv_tail, inv_high, inv_mid, places, hot, mask, lhs, spread, slot_hot, deposit, row_id, turned,
    shapes, lower, shapes_near, pairs_near, slots_near, ghosts, predicted_of,
    rest8, slot8, slot_flat, cells_own, cells_near,
    flow_out, flow_in, force_out, force_in, blocks, edges_out, edges_in, fluid, post, fluid_2, post_2,
    field, field_2,
    in_sem, ready, ring_send, ring_recv, near_send, near_recv, pairs_send, pairs_recv, slots_send, slots_recv, flow_send, flow_recv, force_send, force_recv,
    cells_send, cells_recv, edge_send, edge_recv, block_send, block_recv,
):
    n_brick, n_group, verts, bodies, slot_count = sizes
    me = lax.axis_index("brick")
    group = lax.axis_index("group")
    cx, cy = pop_ref.shape[1:3]
    width = shapes.shape[2]
    blocks_v = width // LANES
    rows_v = bodies * BODY_ROWS
    tiles = pairs.shape[1]
    depth = ITERS
    peer_cells = slot_count // n_brick
    wide = n_brick * GROUP
    wide_tiles = wide // LANES
    slot_tiles = cells_own.shape[1] // LANES
    long_y = cy + 2 * RING
    short_y = cy + 2
    part = cx * long_y
    f32, bf16, i32 = jnp.float32, jnp.bfloat16, jnp.int32

    def brick_at(offset):
        return lax.rem(me + (offset + n_brick), n_brick)

    def group_at(offset):
        return lax.rem(group + (offset + n_group), n_group)

    def iota(shape, axis):
        return lax.broadcasted_iota(i32, shape, axis)

    near = [(dg, o) for dg in (0, 1, -1) for o in range(n_brick) if (dg, o) != (0, 0)]
    first = [(0, o) for o in range(1, n_brick)] + [(1, 0), (-1, 0)]
    barrier = pltpu.get_barrier_semaphore()
    for dg, o in first:
        pl.semaphore_signal(barrier, inc=1, device_id=(group_at(dg), brick_at(o)), device_id_type=MESH)
    loads = [
        pltpu.make_async_copy(source, target, in_sem.at[n])
        for n, (source, target) in enumerate([
            (pop_hbm, pop_ref), (cells_hbm, cells_ref), (pos_hbm, pos_ref), (rest_hbm, rest_in),
            (own_hbm, pairs.at[0]), (far_hbm, pairs.at[1]), (slots_hbm, slots_ref), (inv_hbm, inv_raw),
        ])
    ]
    for load in loads:
        load.start()
    inv_copy = loads.pop()
    for load in loads:
        load.wait()

    def remote(source, target, send, recv, dg, o):
        copy = pltpu.make_async_remote_copy(
            src_ref=source, dst_ref=target, send_sem=send, recv_sem=recv,
            device_id=(group_at(dg), brick_at(o)), device_id_type=MESH,
        )
        copy.start()
        return copy

    def all_bytes(ref, sem):
        pltpu.make_async_copy(ref, ref, sem).wait()

    shapes[0] = jnp.zeros((rows_v, width), f32)
    rest8[...] = jnp.zeros((rows_v, width), f32)
    for b in range(bodies):
        for c in range(3):
            r = b * BODY_ROWS + c
            shapes[0, r : r + 1, 0:verts] = pos_ref[c, b : b + 1, :]
            rest8[r : r + 1, 0:verts] = rest_in[c : c + 1, :]
    cells_own[...] = jnp.zeros(cells_own.shape, i32)
    cells_own[:, 0:slot_count] = cells_ref[...]
    for x in range(cx):
        for i in range(DIRS):
            edges_out[0, i, 2 * x : 2 * x + 2, :] = pop_ref[i, x, 0:RING, :]
            edges_out[1, i, 2 * x : 2 * x + 2, :] = pop_ref[i, x, cy - RING : cy, :]

    lane8 = iota((8, LANES), 1)
    sub8 = iota((8, LANES), 0)
    in_group = lane8 % GROUP
    of_group = lane8 // GROUP

    def sample(flow, step):
        lines = cx * cy
        got = []
        for t in range(slot_tiles):
            cell = cells_own[0:1, t * LANES : (t + 1) * LANES]
            at = jnp.broadcast_to(cell & (LANES - 1), (lines, LANES))
            chosen = jnp.broadcast_to(cell >> 7, (lines, LANES)) == iota((lines, LANES), 0)
            got.append([
                jnp.sum(jnp.where(chosen, take(flow[c], at), 0.0), axis=0, keepdims=True) for c in range(3)
            ])
        for base in range(0, n_brick, 8):
            owner = base + sub8 - in_group // peer_cells
            owner = jnp.where(owner < 0, owner + n_brick, owner)
            slot = owner * peer_cells + in_group % peer_cells
            touched = {(base + n) % n_brick * peer_cells // LANES for n in range(1 - depth, 8)}
            message = jnp.zeros((8, LANES), f32)
            for c in range(3):
                for t in sorted(touched):
                    moved = take(jnp.broadcast_to(got[t][c], (8, LANES)), slot & (LANES - 1))
                    message = jnp.where((of_group == c) & (slot >> 7 == t), moved, message)
            for s in range(8):
                flow_out[step, base + s] = message[s : s + 1, :]

    def send_flow(step):
        pltpu.make_async_copy(flow_out.at[step, me], flow_in.at[step, me], flow_recv.at[step]).start()
        for o in range(1, n_brick):
            remote(
                flow_out.at[step, brick_at(o)], flow_in.at[step, me],
                flow_send.at[step], flow_recv.at[step], 0, o,
            )

    def send_ring(k):
        return remote(shapes.at[k], lower.at[k], ring_send.at[k], ring_recv.at[k], 0, 1)

    lines_own = [
        jnp.concatenate([pop_ref[i, x] for x in range(cx)], axis=0) for i in range(DIRS)
    ]
    density, momentum = moments(lines_own)
    inverse_density = 1.0 / density
    sample([m * inverse_density for m in momentum], 0)

    pl.semaphore_wait(barrier, len(first))
    for dg in (1, -1):
        pl.semaphore_signal(ready, inc=1, device_id=(group_at(dg), brick_at(0)), device_id_type=MESH)
    send_flow(0)
    copies = [send_ring(0)]
    pl.semaphore_wait(ready, 2)
    for n, (dg, db) in enumerate([(a, b) for a in (-1, 0, 1) for b in (-1, 0, 1) if (a, b) != (0, 0)]):
        copies.append(remote(
            cells_own, cells_near.at[1 - dg, 1 - db], cells_send.at[n], cells_recv.at[n], dg, db
        ))
    cells_copies = copies[1:]
    edge_copies = [
        remote(
            edges_out.at[side], edges_in.at[1 - dg, side],
            edge_send.at[dg + 1, side], edge_recv.at[dg + 1, side], dg, 1 if side else -1,
        )
        for dg in (0, -1, 1)
        for side in (0, 1)
    ]
    block_copies = [
        remote(pop_ref, blocks.at[n], block_send.at[n], block_recv.at[n], dg, 0)
        for n, dg in enumerate((1, -1))
    ]

    ghost_copies = []
    for e in range(1, depth):
        ghost_copies.append(remote(
            pairs, pairs_near.at[e - 1], pairs_send.at[e - 1], pairs_recv.at[e - 1], 0, e
        ))
        ghost_copies.append(remote(
            slots_ref, slots_near.at[e - 1], slots_send.at[e - 1], slots_recv.at[e - 1], 0, e
        ))

    def place(index):
        body = jnp.zeros(index.shape, i32)
        for b in range(1, bodies):
            body = body + jnp.where(index >= b * verts, 1, 0)
        vertex = index - body * verts
        return vertex & (LANES - 1), vertex >> 7, body

    lane_square = iota((LANES, LANES), 1)

    def build_pairs(e, ref):
        own_lane, own_block, own_body = place(ref[0])
        far_lane, far_block, far_body = place(ref[1])
        places[e, 0] = own_lane
        places[e, 1] = own_body * blocks_v + own_block
        places[e, 2] = far_lane
        places[e, 3] = far_body * blocks_v + far_block
        turned[e, 0:tiles, :] = own_lane.astype(f32)
        turned[e, tiles:LANES, :] = jnp.zeros((LANES - tiles, LANES), f32)
        columns = jnp.transpose(turned[e]).astype(i32)
        for t in range(tiles):
            column = jnp.broadcast_to(columns[:, t : t + 1], (LANES, LANES))
            hot[e, t * LANES : (t + 1) * LANES, :] = jnp.where(column == lane_square, 1.0, 0.0).astype(bf16)
            chosen = jnp.broadcast_to(own_block[t : t + 1, :], (blocks_v * rows_v, LANES))
            mask[e, t] = jnp.where(
                chosen == iota((blocks_v * rows_v, LANES), 0) // rows_v, 1.0, 0.0
            ).astype(bf16)

    def place_slots(e, ref):
        slot_flat[e, :, 0 : bodies * verts] = ref[...]
        total = slot_flat.shape[2]
        flat = jnp.broadcast_to(slot_flat[e], (8, total))
        picked = flat[:, :width]
        row_body = iota((rows_v, width), 0) // BODY_ROWS
        for b in range(1, bodies):
            moved = pltpu.roll(flat, total - b * verts, 1)[:, :width]
            picked = jnp.where(row_body == b, moved, picked)
        slot8[e] = jnp.where(iota((rows_v, width), 1) < verts, picked, -1)

    slot_flat[...] = jnp.zeros(slot_flat.shape, i32)
    spread[...] = jnp.zeros(spread.shape, f32)
    build_pairs(0, pairs)
    place_slots(0, slots_ref)

    def build_ghosts():
        for copy in ghost_copies:
            copy.wait_recv()
        for e in range(1, depth):
            build_pairs(e, pairs_near.at[e - 1])
            place_slots(e, slots_near.at[e - 1])

    inv_copy.wait()
    chunk = 32
    full = verts // chunk
    edge = verts // LANES * LANES
    for ref in (inv_high, inv_mid):
        ref[:, edge:width] = jnp.zeros((width, width - edge), bf16)
        ref[full * chunk : width, :] = jnp.zeros((width - full * chunk, width), bf16)

    def split(n, _):
        at = pl.multiple_of(n * chunk, chunk)
        high, mid = halves(inv_raw[pl.ds(at, chunk), :])
        inv_high[pl.ds(at, chunk), 0:verts] = high.astype(bf16)
        inv_mid[pl.ds(at, chunk), 0:verts] = mid.astype(bf16)
        return 0

    lax.fori_loop(0, full, split, 0)
    if verts % chunk:
        inv_tail[...] = jnp.zeros(inv_tail.shape, f32)
        inv_tail[0 : verts % chunk, 0:verts] = inv_raw[full * chunk : verts, :]
        high, mid = halves(inv_tail[...])
        inv_high[full * chunk : (full + 1) * chunk, :] = high.astype(bf16)
        inv_mid[full * chunk : (full + 1) * chunk, :] = mid.astype(bf16)

    def pick(ref, lane, ident):
        total = [jnp.zeros((tiles, LANES), f32)] * 3
        for b in range(bodies):
            for h in range(blocks_v):
                chosen = ident == b * blocks_v + h
                for c in range(3):
                    r = b * BODY_ROWS + c
                    row = ref[r : r + 1, h * LANES : (h + 1) * LANES]
                    got = take(jnp.broadcast_to(row, (tiles, LANES)), lane)
                    total[c] = jnp.where(chosen, got, total[c])
        return total

    def contact(e, shape_of, lower_of, before_far):
        own_id = places[e, 1]
        own = pick(shape_of, places[e, 0], own_id)
        before_far()
        far = pick(lower_of, places[e, 2], places[e, 3])
        diff = [a - b for a, b in zip(own, far)]
        square = diff[0] * diff[0] + diff[1] * diff[1] + diff[2] * diff[2]
        scale = contact_gain * jnp.exp(-square / contact_range)
        for b in range(bodies):
            inside = (own_id >= b * blocks_v) & (own_id < (b + 1) * blocks_v)
            for c in range(3):
                r = b * BODY_ROWS + c
                spread[e, r * tiles : (r + 1) * tiles, :] = jnp.where(inside, scale * diff[c], 0.0)
        half = blocks_v * rows_v
        for t in range(tiles):
            push = spread[e, pl.ds(t, rows_v, stride=tiles), :]
            for n, piece in enumerate(halves(push)):
                pair = jnp.concatenate([piece, piece], axis=0).astype(bf16)
                lhs[e, n * half : (n + 1) * half, t * LANES : (t + 1) * LANES] = (
                    jnp.concatenate([pair] * (blocks_v // 2), axis=0) * mask[e, t]
                )
        middle = tiles // 2 * LANES
        added = jnp.dot(lhs[e, :, :middle], hot[e, :middle], preferred_element_type=f32)
        added = added + jnp.dot(lhs[e, :, middle:], hot[e, middle:], preferred_element_type=f32)
        added = added[:half] + added[half:]
        return jnp.concatenate([added[h * rows_v : (h + 1) * rows_v] for h in range(blocks_v)], axis=1)

    copies_ring = {0: copies[0]}

    def received(step, e):
        out = []
        per_tile = LANES // peer_cells
        for t in range(slot_tiles):
            index = (sub8 % BODY_ROWS) * GROUP + e * peer_cells + lane8 % peer_cells
            table = jnp.zeros((8, LANES), f32)
            for s in range(t * per_tile, min((t + 1) * per_tile, n_brick)):
                moved = take(jnp.broadcast_to(flow_in[step, s], (8, LANES)), index)
                table = jnp.where(lane8 // peer_cells == s % per_tile, moved, table)
            out.append(table)
        return out

    def vertex_flow(step, e):
        tables = received(step, e)
        parts = []
        for h in range(blocks_v):
            slot = jnp.maximum(slot8[e, :, h * LANES : (h + 1) * LANES], 0)
            got = take(tables[0], slot & (LANES - 1))
            for t in range(1, slot_tiles):
                got = jnp.where(slot >> 7 == t, take(tables[t], slot & (LANES - 1)), got)
            parts.append(got)
        return jnp.concatenate(parts, axis=1)

    def relax(cases):
        high, mid = [], []
        for shape, predicted, touch in cases:
            centroid = jnp.sum(shape, axis=1, keepdims=True) * (1.0 / verts)
            rhs = mass_weight * predicted + shape_weight * (centroid + rest8[...]) + touch
            a, b = halves(rhs)
            high.append(a)
            mid.append(b)
        if len(cases) % 2:
            high.append(jnp.zeros((rows_v, width), f32))
            mid.append(jnp.zeros((rows_v, width), f32))
        count = len(high) * rows_v
        high = jnp.concatenate(high, axis=0).astype(bf16)
        left = jnp.concatenate([high, jnp.concatenate(mid, axis=0).astype(bf16)], axis=0)
        both = jnp.dot(left, inv_high[...], preferred_element_type=f32)
        rest = jnp.dot(high, inv_mid[...], preferred_element_type=f32)
        both = both[:count] + both[count:] + rest
        return [both[n * rows_v : (n + 1) * rows_v] for n in range(len(cases))]

    def build_slots():
        column_of = []
        for h in range(blocks_v):
            rows = slot8[0, :, h * LANES : (h + 1) * LANES].astype(f32)
            turned[0, h * rows_v : (h + 1) * rows_v, :] = rows
        columns = jnp.transpose(turned[0]).astype(i32)
        for t in range(wide_tiles):
            q = iota((LANES, LANES), 1)
            brick = q // GROUP + t * (LANES // GROUP)
            inner = q % GROUP
            target = brick - 1 + inner // peer_cells
            target = jnp.where(target < 0, target + n_brick, target)
            target = jnp.where(target >= n_brick, target - n_brick, target)
            slot = jnp.where(inner < 3 * peer_cells, target * peer_cells + inner % peer_cells, -2)
            for b in range(bodies):
                for h in range(blocks_v):
                    at = h * rows_v + b * BODY_ROWS
                    column = jnp.broadcast_to(columns[:, at : at + 1], (LANES, LANES))
                    slot_hot[b, h * LANES : (h + 1) * LANES, t * LANES : (t + 1) * LANES] = jnp.where(
                        column == slot, 1.0, 0.0
                    ).astype(bf16)

    def build_deposit():
        for copy in cells_copies:
            copy.wait_recv()
        per_tile = LANES // GROUP
        for dg in range(3):
            for t in range(wide_tiles):
                start = t * per_tile * peer_cells
                source, offset = start // LANES, start % LANES
                index = offset + of_group * peer_cells + in_group % peer_cells
                side = in_group // peer_cells
                cell = jnp.zeros((8, LANES), i32)
                for db in range(3):
                    ref = cells_own if (dg, db) == (1, 1) else cells_near.at[dg, db]
                    row = ref[0:1, source * LANES : (source + 1) * LANES]
                    moved = take(jnp.broadcast_to(row, (8, LANES)), index)
                    cell = jnp.where(side == db, moved, cell)
                line = cell >> 7
                x = jnp.zeros((8, LANES), i32)
                for edge_x in range(1, cx):
                    x = x + jnp.where(line >= edge_x * cy, 1, 0)
                y = line - x * cy + cy * (side - 1) + RING
                inside = (y >= 0) & (y < long_y) & (side < 3)
                at = dg * wide_tiles + t
                row_id[dg, :, t * LANES : (t + 1) * LANES] = jnp.where(inside, x * long_y + y, -1)
                turned[1, at : at + 1, :] = (cell & (LANES - 1))[0:1, :].astype(f32)
        columns = jnp.transpose(turned[1]).astype(i32)
        for dg in range(3):
            for t in range(wide_tiles):
                at = dg * wide_tiles + t
                column = jnp.broadcast_to(columns[:, at : at + 1], (LANES, LANES))
                deposit[dg, t * LANES : (t + 1) * LANES, :] = jnp.where(
                    column == lane_square, 1.0, 0.0
                ).astype(bf16)

    def build_fluid():
        for copy in edge_copies + block_copies:
            copy.wait_recv()
        for i in range(DIRS):
            for dg in range(3):
                source = pop_ref if dg == 1 else blocks.at[0 if dg == 0 else 1]
                for x in range(cx):
                    at = (dg * cx + x) * long_y
                    fluid[i, at + RING : at + RING + cy, :] = source[i, x]
                    fluid[i, at + RING + cy : at + long_y, :] = edges_in[dg, 0, i, 2 * x : 2 * x + 2, :]
                    fluid[i, at : at + RING, :] = edges_in[dg, 1, i, 2 * x : 2 * x + 2, :]

    def send_force(predicted, shape, step):
        change = coupling_gain * (shape - predicted)
        left = jnp.concatenate(halves(change), axis=0).astype(bf16)
        total = None
        for b in range(bodies):
            got = jnp.dot(left, slot_hot[b], preferred_element_type=f32)
            got = got[:rows_v] + got[rows_v:]
            if b:
                got = pltpu.roll(got, rows_v - b * BODY_ROWS, 0)
            total = got if total is None else total + got
        per_tile = LANES // GROUP
        index = (sub8 % per_tile) * GROUP + in_group
        for base in range(0, n_brick, 8):
            message = jnp.zeros((8, LANES), f32)
            for c in range(3):
                for n in range(8 // per_tile):
                    t = base // per_tile + n
                    row = total[c : c + 1, t * LANES : (t + 1) * LANES]
                    moved = take(jnp.broadcast_to(row, (8, LANES)), index)
                    chosen = (of_group == c) & (sub8 // per_tile == n)
                    message = jnp.where(chosen, moved, message)
            for s in range(8):
                force_out[step, base + s] = message[s : s + 1, :]
        pltpu.make_async_copy(
            force_out.at[step, me], force_in.at[step, n_brick + me], force_recv.at[step]
        ).start()
        for dg, o in near:
            remote(
                force_out.at[step, brick_at(o)], force_in.at[step, (1 - dg) * n_brick + me],
                force_send.at[step], force_recv.at[step], dg, o,
            )

    def gather_force(step):
        all_bytes(force_in.at[step], force_recv.at[step])
        per_tile = LANES // GROUP
        index = jnp.minimum(sub8, 3) * GROUP + in_group
        for dg in range(3):
            parts = []
            for t in range(wide_tiles):
                table = jnp.zeros((8, LANES), f32)
                for n in range(per_tile):
                    row = force_in[step, dg * n_brick + t * per_tile + n]
                    moved = take(jnp.broadcast_to(row, (8, LANES)), index)
                    table = jnp.where(of_group == n, moved, table)
                parts.append(table)
            table = jnp.concatenate(parts, axis=1)
            ids = jnp.broadcast_to(row_id[dg, 0:1, :], (part, wide))
            chosen = ids == iota((part, wide), 0)
            left = []
            pieces = halves(table)
            for c in range(3):
                for piece in pieces:
                    row = jnp.broadcast_to(piece[c : c + 1, :], (part, wide))
                    left.append(jnp.where(chosen, row, 0.0))
            left = jnp.concatenate(left, axis=0).astype(bf16)
            got = jnp.dot(left, deposit[dg], preferred_element_type=f32)
            for c in range(3):
                field[c, dg * part : (dg + 1) * part, :] = (
                    got[2 * c * part : (2 * c + 1) * part] + got[(2 * c + 1) * part : (2 * c + 2) * part]
                )

    def nothing():
        pass

    background = {1: build_slots, 2: build_deposit, 3: build_fluid}

    def ring_contact(k):
        def wait():
            background.get(k, nothing)()
            copies_ring[k].wait_recv()

        return contact(0, shapes.at[k], lower.at[k], wait)

    touch = ring_contact(0)
    all_bytes(flow_in.at[0], flow_recv.at[0])
    predicted = shapes[0] + time_step * vertex_flow(0, 0)
    for k in range(ITERS):
        (shape,) = relax([(shapes[k], predicted, touch)])
        shapes[k + 1] = shape
        if k < ITERS - 1:
            copies_ring[k + 1] = send_ring(k + 1)
            touch = ring_contact(k + 1)
    send_force(predicted, shape, 0)
    near_copies = [
        remote(shapes.at[ITERS], shapes_near.at[e - 1], near_send.at[e - 1], near_recv.at[e - 1], 0, e)
        for e in range(1, depth + 1)
    ]
    build_ghosts()
    gather_force(0)
    for q in range(3 * part // 8):
        rows = slice(8 * q, 8 * q + 8)
        after = collide([fluid[i, rows, :] for i in range(DIRS)], [field[c, rows, :] for c in range(3)])
        for i in range(DIRS):
            post[i, rows, :] = roll_z(after[i], i)
    for i in range(DIRS):
        step_x, step_y, _ = velocities[i]
        for x in range(cx + 2):
            at = (x + 1 - step_x) * long_y + 1 - step_y
            fluid_2[i, x * short_y : (x + 1) * short_y, :] = post[i, at : at + short_y, :]
    lines_own = [
        jnp.concatenate(
            [fluid_2[i, (x + 1) * short_y + 1 : (x + 1) * short_y + 1 + cy, :] for x in range(cx)], axis=0
        )
        for i in range(DIRS)
    ]
    density, momentum = moments(lines_own)
    inverse_density = 1.0 / density
    sample([m * inverse_density for m in momentum], 1)
    send_flow(1)

    for copy in near_copies:
        copy.wait_recv()
    level = [shapes.at[ITERS]] + [shapes_near.at[e - 1] for e in range(1, depth + 1)]
    touches = [contact(e, level[e], level[e + 1], nothing) for e in range(depth)]
    all_bytes(flow_in.at[1], flow_recv.at[1])
    for e in range(depth):
        predicted_of[e] = level[e][...] + time_step * vertex_flow(1, e)
    for sweep in range(ITERS):
        count = ITERS - sweep
        made = relax([(level[e][...], predicted_of[e], touches[e]) for e in range(count)])
        for e in range(count):
            ghosts[sweep, e] = made[e]
        level = [ghosts.at[sweep, e] for e in range(count)]
        touches = [contact(e, level[e], level[e + 1], nothing) for e in range(count - 1)]
    send_force(predicted_of[0], made[0], 1)

    for b in range(bodies):
        for c in range(3):
            r = b * BODY_ROWS + c
            outp_ref[c, b : b + 1, :] = ghosts[ITERS - 1, 0, r : r + 1, 0:verts]
    gather_force(1)
    for c in range(3):
        for x in range(cx + 2):
            at = (x + 1) * long_y + 1
            field_2[c, x * short_y : (x + 1) * short_y, :] = field[c, at : at + short_y, :]
    for q in range((cx + 2) * short_y // 8):
        rows = slice(8 * q, 8 * q + 8)
        after = collide([fluid_2[i, rows, :] for i in range(DIRS)], [field_2[c, rows, :] for c in range(3)])
        for i in range(DIRS):
            post_2[i, rows, :] = roll_z(after[i], i)
    for i in range(DIRS):
        step_x, step_y, _ = velocities[i]
        for x in range(cx):
            at = (x + 1 - step_x) * short_y + 1 - step_y
            outf_ref[i, x] = post_2[i, at : at + cy, :]

    for copy in copies_ring.values():
        copy.wait_send()
    for copy in cells_copies + edge_copies + block_copies + ghost_copies + near_copies:
        copy.wait_send()
    for step in range(STEPS):
        all_bytes(flow_out.at[step, pl.ds(0, n_brick - 1)], flow_send.at[step])
        all_bytes(force_in.at[step, pl.ds(0, 3 * n_brick - 1)], force_send.at[step])


def on_device(
    populations, positions, rest_shape, inverse, sample_cells, vertex_slots, pair_own, pair_far
):
    n_brick = lax.axis_size("brick")
    n_group = lax.axis_size("group")
    slot_count = sample_cells.shape[1]
    bodies, verts = positions.shape[1:]
    width = up(verts, LANES)
    rows = bodies * BODY_ROWS
    dirs, cx, cy, lanes = populations.shape
    tiles = pair_own.shape[1] // LANES
    wide = n_brick * GROUP
    long_rows = 3 * cx * (cy + 2 * RING)
    short_rows = (cx + 2) * (cy + 2)
    blocks_v = width // LANES
    f32, bf16, i32 = jnp.float32, jnp.bfloat16, jnp.int32
    vmem = pltpu.VMEM
    dma = pltpu.SemaphoreType.DMA
    in_vmem = pl.BlockSpec(memory_space=pltpu.VMEM)
    return pl.pallas_call(
        functools.partial(step_kernel, (n_brick, n_group, verts, bodies, slot_count)),
        out_shape=(
            jax.ShapeDtypeStruct(populations.shape, f32),
            jax.ShapeDtypeStruct(positions.shape, f32),
        ),
        in_specs=[pl.BlockSpec(memory_space=pl.ANY)] * 8,
        out_specs=(in_vmem, in_vmem),
        scratch_shapes=[
            vmem(populations.shape, f32),
            vmem(positions.shape, f32),
            vmem(rest_shape.shape, f32),
            vmem(sample_cells.shape, i32),
            vmem(vertex_slots.shape, i32),
            vmem((2, tiles, LANES), i32),
            vmem((verts, verts), f32),
            vmem((32, width), f32),
            vmem((width, width), bf16),
            vmem((width, width), bf16),
            vmem((ITERS, 4, tiles, LANES), i32),
            vmem((ITERS, tiles * LANES, LANES), bf16),
            vmem((ITERS, tiles, blocks_v * rows, LANES), bf16),
            vmem((ITERS, 2 * blocks_v * rows, tiles * LANES), bf16),
            vmem((ITERS, rows * tiles, LANES), f32),
            vmem((bodies, width, wide), bf16),
            vmem((3, wide, LANES), bf16),
            vmem((3, 8, wide), i32),
            vmem((ITERS, LANES, LANES), f32),
            vmem((ITERS + 1, rows, width), f32),
            vmem((ITERS, rows, width), f32),
            vmem((ITERS, rows, width), f32),
            vmem((ITERS - 1, 2, tiles, LANES), i32),
            vmem((ITERS - 1,) + vertex_slots.shape, i32),
            vmem((ITERS, ITERS, rows, width), f32),
            vmem((ITERS, rows, width), f32),
            vmem((rows, width), f32),
            vmem((ITERS, rows, width), i32),
            vmem((ITERS, 1, up(bodies * verts + width, LANES)), i32),
            vmem((1, up(slot_count, LANES)), i32),
            vmem((3, 3, 1, up(slot_count, LANES)), i32),
            vmem((STEPS, n_brick, 1, LANES), f32),
            vmem((STEPS, n_brick, 1, LANES), f32),
            vmem((STEPS, n_brick, 1, LANES), f32),
            vmem((STEPS, 3 * n_brick, 1, LANES), f32),
            vmem((2,) + populations.shape, f32),
            vmem((2, dirs, 2 * cx, LANES), f32),
            vmem((3, 2, dirs, 2 * cx, LANES), f32),
            vmem((dirs, long_rows, LANES), f32),
            vmem((dirs, long_rows, LANES), f32),
            vmem((dirs, short_rows, LANES), f32),
            vmem((dirs, short_rows, LANES), f32),
            vmem((3, long_rows, LANES), f32),
            vmem((3, short_rows, LANES), f32),
            dma((8,)),
            pltpu.SemaphoreType.REGULAR,
            dma((ITERS,)),
            dma((ITERS,)),
            dma((ITERS,)),
            dma((ITERS,)),
            dma((ITERS - 1,)),
            dma((ITERS - 1,)),
            dma((ITERS - 1,)),
            dma((ITERS - 1,)),
            dma((STEPS,)),
            dma((STEPS,)),
            dma((STEPS,)),
            dma((STEPS,)),
            dma((8,)),
            dma((8,)),
            dma((3, 2)),
            dma((3, 2)),
            dma((2,)),
            dma((2,)),
        ],
        compiler_params=pltpu.CompilerParams(
            collective_id=0, has_side_effects=True, vmem_limit_bytes=60 * 1024 * 1024
        ),
    )(
        populations, positions, rest_shape, inverse, sample_cells, vertex_slots,
        pair_own.reshape(tiles, LANES), pair_far.reshape(tiles, LANES),
    )


def solution(mesh):
    placed = (
        P(None, "group", "brick", None),
        P(None, ("group", "brick"), None),
        P(),
        P(),
        P(("group", "brick"), None),
        P(("group", "brick"), None),
        P(("group", "brick"), None),
        P(("group", "brick"), None),
    )
    return jax.shard_map(
        on_device,
        mesh=mesh,
        in_specs=placed,
        out_specs=(P(None, "group", "brick", None), P(None, ("group", "brick"), None)),
        check_vma=False,
    )
```

```python
import functools

import jax
import jax.numpy as jnp
from jax import lax
from jax.experimental import pallas as pl
from jax.experimental.pallas import tpu as pltpu
from jax.sharding import PartitionSpec as P

ITERS = 4
STEPS = 2

velocities = [
    (0, 0, 0),
    (0, 0, 1),
    (0, 0, -1),
    (1, 0, 0),
    (-1, 0, 0),
    (0, 1, 0),
    (0, -1, 0),
    (1, 1, 0),
    (-1, -1, 0),
    (1, -1, 0),
    (-1, 1, 0),
    (1, 0, 1),
    (-1, 0, -1),
    (1, 0, -1),
    (-1, 0, 1),
    (0, 1, 1),
    (0, -1, -1),
    (0, 1, -1),
    (0, -1, 1),
]
weights_table = [1.0 / 3.0] + [1.0 / 18.0] * 6 + [1.0 / 36.0] * 12
DIRS = len(velocities)
relax_time = 0.8
contact_gain = 0.5
contact_range = 6.0
coupling_gain = 0.05
mass_weight = 1.0
shape_weight = 1.0
time_step = 1.0

LANES = 128
BODY_ROWS = 4
GROUP = 32
RING = 2
MESH = pl.DeviceIdType.MESH


def up(value, unit):
    return -(-value // unit) * unit


def take(rows, index):
    return jnp.take_along_axis(rows, index, axis=1, mode="promise_in_bounds")


def halves(value):
    high = value.astype(jnp.bfloat16).astype(jnp.float32)
    return high, value - high


def signed_sum(terms, axis):
    total = None
    for p in range(1, DIRS, 2):
        sign = velocities[p][axis]
        if sign == 0:
            continue
        if total is None:
            assert sign > 0
            total = terms[p]
        else:
            total = total + terms[p] if sign > 0 else total - terms[p]
    return total


def moments(rows):
    density = functools.reduce(lambda a, b: a + b, rows)
    opposite = {p: rows[p] - rows[p + 1] for p in range(1, DIRS, 2)}
    return density, [signed_sum(opposite, axis) for axis in range(3)]


def dot_c(vector, p):
    total = None
    for axis in range(3):
        sign = velocities[p][axis]
        if sign == 0:
            continue
        if total is None:
            total = vector[axis] if sign > 0 else -vector[axis]
        else:
            total = total + vector[axis] if sign > 0 else total - vector[axis]
    return total


def collide(rows, force):
    density, momentum = moments(rows)
    inverse_density = 1.0 / density
    veloc = [(momentum[a] + 0.5 * force[a]) * inverse_density for a in range(3)]
    square = veloc[0] * veloc[0] + veloc[1] * veloc[1] + veloc[2] * veloc[2]
    keep, gain = 1.0 - 1.0 / relax_time, 1.0 / relax_time
    base = 1.0 - 1.5 * square
    scaled = [density * (gain * w) for w in (1.0 / 3.0, 1.0 / 18.0, 1.0 / 36.0)]
    out = [None] * DIRS
    out[0] = keep * rows[0] + scaled[0] * base
    for p in range(1, DIRS, 2):
        weight = weights_table[p]
        rho = scaled[1] if p < 7 else scaled[2]
        along = dot_c(veloc, p)
        even = rho * (base + 4.5 * (along * along))
        odd = rho * (3.0 * along) + (3.0 * weight) * dot_c(force, p)
        out[p] = keep * rows[p] + (even + odd)
        out[p + 1] = keep * rows[p + 1] + (even - odd)
    return out


def roll_z(value, index):
    step = velocities[index][2]
    if step == 0:
        return value
    return pltpu.roll(value, step % LANES, 1)


def step_kernel(
    sizes, pop_hbm, pos_hbm, rest_hbm, inv_hbm, cells_hbm, slots_hbm, own_hbm, far_hbm,
    outf_ref, outp_ref,
    pop_ref, pos_ref, rest_in, cells_ref, slots_ref, pairs,
    inv_raw, inv_tail, inv_high, inv_mid, inv_last, places, hot, mask, lhs, spread, slot_hot, deposit, row_id, turned,
    shapes, lower, under, shapes_near, pairs_near, slots_near, ghosts, predicted_of,
    rest8, slot8, slot_flat, cells_own, cells_near,
    flow_out, flow_in, force_out, force_in, blocks, edges_out, edges_in, fluid, post, fluid_2, post_2,
    field, field_2,
    in_sem, ready, ring_send, ring_recv, near_send, near_recv, pairs_send, pairs_recv, slots_send, slots_recv, flow_send, flow_recv, force_send, force_recv,
    cells_send, cells_recv, edge_send, edge_recv, block_send, block_recv,
):
    n_brick, n_group, verts, bodies, slot_count = sizes
    me = lax.axis_index("brick")
    group = lax.axis_index("group")
    cx, cy = pop_ref.shape[1:3]
    width = shapes.shape[2]
    blocks_v = width // LANES
    rows_v = bodies * BODY_ROWS
    tiles = pairs.shape[1]
    depth = ITERS
    peer_cells = slot_count // n_brick
    wide = n_brick * GROUP
    wide_tiles = wide // LANES
    slot_tiles = cells_own.shape[1] // LANES
    long_y = cy + 2 * RING
    short_y = cy + 2
    part = cx * long_y
    f32, bf16, i32 = jnp.float32, jnp.bfloat16, jnp.int32

    def brick_at(offset):
        return lax.rem(me + (offset + n_brick), n_brick)

    def group_at(offset):
        return lax.rem(group + (offset + n_group), n_group)

    def iota(shape, axis):
        return lax.broadcasted_iota(i32, shape, axis)

    near = [(dg, o) for dg in (0, 1, -1) for o in range(n_brick) if (dg, o) != (0, 0)]
    first = [(0, o) for o in range(1, n_brick)] + [(1, 0), (-1, 0)]
    barrier = pltpu.get_barrier_semaphore()
    for dg, o in first:
        pl.semaphore_signal(barrier, inc=1, device_id=(group_at(dg), brick_at(o)), device_id_type=MESH)
    loads = [
        pltpu.make_async_copy(source, target, in_sem.at[n])
        for n, (source, target) in enumerate([
            (pop_hbm, pop_ref), (cells_hbm, cells_ref), (pos_hbm, pos_ref), (rest_hbm, rest_in),
            (own_hbm, pairs.at[0]), (far_hbm, pairs.at[1]), (slots_hbm, slots_ref), (inv_hbm, inv_raw),
        ])
    ]
    for load in loads:
        load.start()
    inv_copy = loads.pop()
    for load in loads:
        load.wait()

    def remote(source, target, send, recv, dg, o):
        copy = pltpu.make_async_remote_copy(
            src_ref=source, dst_ref=target, send_sem=send, recv_sem=recv,
            device_id=(group_at(dg), brick_at(o)), device_id_type=MESH,
        )
        copy.start()
        return copy

    def all_bytes(ref, sem):
        pltpu.make_async_copy(ref, ref, sem).wait()

    shapes[0] = jnp.zeros((rows_v, width), f32)
    rest8[...] = jnp.zeros((rows_v, width), f32)
    for b in range(bodies):
        for c in range(3):
            r = b * BODY_ROWS + c
            shapes[0, r : r + 1, 0:verts] = pos_ref[c, b : b + 1, :]
            rest8[r : r + 1, 0:verts] = rest_in[c : c + 1, :]
    cells_own[...] = jnp.zeros(cells_own.shape, i32)
    cells_own[:, 0:slot_count] = cells_ref[...]
    for x in range(cx):
        for i in range(DIRS):
            edges_out[0, i, 2 * x : 2 * x + 2, :] = pop_ref[i, x, 0:RING, :]
            edges_out[1, i, 2 * x : 2 * x + 2, :] = pop_ref[i, x, cy - RING : cy, :]

    lane8 = iota((8, LANES), 1)
    sub8 = iota((8, LANES), 0)
    in_group = lane8 % GROUP
    of_group = lane8 // GROUP

    def sample(flow, step):
        lines = cx * cy
        got = []
        for t in range(slot_tiles):
            cell = cells_own[0:1, t * LANES : (t + 1) * LANES]
            at = jnp.broadcast_to(cell & (LANES - 1), (lines, LANES))
            chosen = jnp.broadcast_to(cell >> 7, (lines, LANES)) == iota((lines, LANES), 0)
            got.append([
                jnp.sum(jnp.where(chosen, take(flow[c], at), 0.0), axis=0, keepdims=True) for c in range(3)
            ])
        for base in range(0, n_brick, 8):
            owner = base + sub8 - in_group // peer_cells
            owner = jnp.where(owner < 0, owner + n_brick, owner)
            slot = owner * peer_cells + in_group % peer_cells
            touched = {(base + n) % n_brick * peer_cells // LANES for n in range(1 - depth, 8)}
            message = jnp.zeros((8, LANES), f32)
            for c in range(3):
                for t in sorted(touched):
                    moved = take(jnp.broadcast_to(got[t][c], (8, LANES)), slot & (LANES - 1))
                    message = jnp.where((of_group == c) & (slot >> 7 == t), moved, message)
            for s in range(8):
                flow_out[step, base + s] = message[s : s + 1, :]

    def send_flow(step):
        pltpu.make_async_copy(flow_out.at[step, me], flow_in.at[step, me], flow_recv.at[step]).start()
        for o in range(1, n_brick):
            remote(
                flow_out.at[step, brick_at(o)], flow_in.at[step, me],
                flow_send.at[step], flow_recv.at[step], 0, o,
            )

    def send_shapes(n):
        return [
            remote(
                shapes.at[2 * n], lower.at[n, e - 1], ring_send.at[n, e - 1], ring_recv.at[n, e - 1], 0, e
            )
            for e in (1, 2)
        ]

    def send_pairs(e):
        return remote(pairs, pairs_near.at[e - 1], pairs_send.at[e - 1], pairs_recv.at[e - 1], 0, e)

    def send_slots(e):
        return remote(slots_ref, slots_near.at[e - 1], slots_send.at[e - 1], slots_recv.at[e - 1], 0, e)

    lines_own = [
        jnp.concatenate([pop_ref[i, x] for x in range(cx)], axis=0) for i in range(DIRS)
    ]
    density, momentum = moments(lines_own)
    inverse_density = 1.0 / density
    sample([m * inverse_density for m in momentum], 0)

    pl.semaphore_wait(barrier, len(first))
    for dg in (1, -1):
        pl.semaphore_signal(ready, inc=1, device_id=(group_at(dg), brick_at(0)), device_id_type=MESH)
    send_flow(0)
    start_copies = send_shapes(0)
    ghost_copies = [send_pairs(1), send_slots(1)]
    for e in range(2, depth):
        ghost_copies += [send_pairs(e), send_slots(e)]

    def place(index):
        body = jnp.zeros(index.shape, i32)
        for b in range(1, bodies):
            body = body + jnp.where(index >= b * verts, 1, 0)
        vertex = index - body * verts
        return vertex & (LANES - 1), vertex >> 7, body

    lane_square = iota((LANES, LANES), 1)

    def build_pairs(e, ref):
        own_lane, own_block, own_body = place(ref[0])
        far_lane, far_block, far_body = place(ref[1])
        places[e, 0] = own_lane
        places[e, 1] = own_body * blocks_v + own_block
        places[e, 2] = far_lane
        places[e, 3] = far_body * blocks_v + far_block
        turned[e, 0:tiles, :] = own_lane.astype(f32)
        turned[e, tiles:LANES, :] = jnp.zeros((LANES - tiles, LANES), f32)
        columns = jnp.transpose(turned[e]).astype(i32)
        for t in range(tiles):
            column = jnp.broadcast_to(columns[:, t : t + 1], (LANES, LANES))
            hot[e, t * LANES : (t + 1) * LANES, :] = jnp.where(column == lane_square, 1.0, 0.0).astype(bf16)
            chosen = jnp.broadcast_to(own_block[t : t + 1, :], (blocks_v * rows_v, LANES))
            mask[e, t] = jnp.where(
                chosen == iota((blocks_v * rows_v, LANES), 0) // rows_v, 1.0, 0.0
            ).astype(bf16)

    def place_slots(e, ref):
        slot_flat[e, :, 0 : bodies * verts] = ref[...]
        total = slot_flat.shape[2]
        flat = jnp.broadcast_to(slot_flat[e], (8, total))
        picked = flat[:, :width]
        row_body = iota((rows_v, width), 0) // BODY_ROWS
        for b in range(1, bodies):
            moved = pltpu.roll(flat, total - b * verts, 1)[:, :width]
            picked = jnp.where(row_body == b, moved, picked)
        slot8[e] = jnp.where(iota((rows_v, width), 1) < verts, picked, -1)

    slot_flat[...] = jnp.zeros(slot_flat.shape, i32)
    spread[...] = jnp.zeros(spread.shape, f32)
    build_pairs(0, pairs)
    place_slots(0, slots_ref)

    def build_ghosts():
        for copy in ghost_copies[2:]:
            copy.wait_recv()
        for e in range(2, depth):
            build_pairs(e, pairs_near.at[e - 1])
            place_slots(e, slots_near.at[e - 1])

    inv_copy.wait()
    chunk = 32
    edge = verts // LANES * LANES
    tail = verts - edge
    main = inv_high.shape[1]
    inv_tail[...] = jnp.zeros(inv_tail.shape, f32)
    inv_tail[0:tail, 0:verts] = inv_raw[edge:verts, :]

    def split(n, _):
        at = pl.multiple_of(n * chunk, chunk)
        high, mid = halves(inv_raw[pl.ds(at, chunk), 0:edge])
        high = high.astype(bf16)
        mid = mid.astype(bf16)
        inv_high[pl.ds(at, chunk), :] = high[:, :main]
        inv_mid[pl.ds(at, chunk), :] = mid[:, :main]
        inv_last[pl.ds(at, chunk), 0 : edge - main] = high[:, main:]
        inv_last[pl.ds(at, chunk), edge - main : 2 * (edge - main)] = mid[:, main:]
        return 0

    lax.fori_loop(0, edge // chunk, split, 0)

    pl.semaphore_wait(ready, 2)
    cells_copies = []
    for n, (dg, db) in enumerate([(a, b) for a in (-1, 0, 1) for b in (-1, 0, 1) if (a, b) != (0, 0)]):
        cells_copies.append(remote(
            cells_own, cells_near.at[1 - dg, 1 - db], cells_send.at[n], cells_recv.at[n], dg, db
        ))
    edge_copies = [
        remote(
            edges_out.at[side], edges_in.at[1 - dg, side],
            edge_send.at[dg + 1, side], edge_recv.at[dg + 1, side], dg, 1 if side else -1,
        )
        for dg in (0, -1, 1)
        for side in (0, 1)
    ]
    block_copies = [
        remote(pop_ref, blocks.at[n], block_send.at[n], block_recv.at[n], dg, 0)
        for n, dg in enumerate((1, -1))
    ]


    def pick(ref, lane, ident):
        total = [jnp.zeros((tiles, LANES), f32)] * 3
        for b in range(bodies):
            for h in range(blocks_v):
                chosen = ident == b * blocks_v + h
                for c in range(3):
                    r = b * BODY_ROWS + c
                    row = ref[r : r + 1, h * LANES : (h + 1) * LANES]
                    got = take(jnp.broadcast_to(row, (tiles, LANES)), lane)
                    total[c] = jnp.where(chosen, got, total[c])
        return total

    def contact(e, shape_of, lower_of, before_far):
        own_id = places[e, 1]
        own = pick(shape_of, places[e, 0], own_id)
        before_far()
        far = pick(lower_of, places[e, 2], places[e, 3])
        diff = [a - b for a, b in zip(own, far)]
        square = diff[0] * diff[0] + diff[1] * diff[1] + diff[2] * diff[2]
        scale = contact_gain * jnp.exp(-square / contact_range)
        for b in range(bodies):
            inside = (own_id >= b * blocks_v) & (own_id < (b + 1) * blocks_v)
            for c in range(3):
                r = b * BODY_ROWS + c
                spread[e, r * tiles : (r + 1) * tiles, :] = jnp.where(inside, scale * diff[c], 0.0)
        half = blocks_v * rows_v
        for t in range(tiles):
            push = spread[e, pl.ds(t, rows_v, stride=tiles), :]
            for n, piece in enumerate(halves(push)):
                pair = jnp.concatenate([piece, piece], axis=0).astype(bf16)
                lhs[e, n * half : (n + 1) * half, t * LANES : (t + 1) * LANES] = (
                    jnp.concatenate([pair] * (blocks_v // 2), axis=0) * mask[e, t]
                )
        middle = tiles // 2 * LANES
        added = jnp.dot(lhs[e, :, :middle], hot[e, :middle], preferred_element_type=f32)
        added = added + jnp.dot(lhs[e, :, middle:], hot[e, middle:], preferred_element_type=f32)
        added = added[:half] + added[half:]
        return jnp.concatenate([added[h * rows_v : (h + 1) * rows_v] for h in range(blocks_v)], axis=1)

    def received(step, e):
        out = []
        per_tile = LANES // peer_cells
        for t in range(slot_tiles):
            index = (sub8 % BODY_ROWS) * GROUP + e * peer_cells + lane8 % peer_cells
            table = jnp.zeros((8, LANES), f32)
            for s in range(t * per_tile, min((t + 1) * per_tile, n_brick)):
                moved = take(jnp.broadcast_to(flow_in[step, s], (8, LANES)), index)
                table = jnp.where(lane8 // peer_cells == s % per_tile, moved, table)
            out.append(table)
        return out

    def vertex_flow(step, e):
        tables = received(step, e)
        parts = []
        for h in range(blocks_v):
            slot = jnp.maximum(slot8[e, :, h * LANES : (h + 1) * LANES], 0)
            got = take(tables[0], slot & (LANES - 1))
            for t in range(1, slot_tiles):
                got = jnp.where(slot >> 7 == t, take(tables[t], slot & (LANES - 1)), got)
            parts.append(got)
        return jnp.concatenate(parts, axis=1)

    def relax(cases):
        high, mid, ends = [], [], []
        for shape, predicted, touch in cases:
            centroid = jnp.sum(shape, axis=1, keepdims=True) * (1.0 / verts)
            rhs = mass_weight * predicted + shape_weight * (centroid + rest8[...]) + touch
            a, b = halves(rhs[:, :edge])
            high.append(a)
            mid.append(b)
            more = jnp.zeros((rows_v, edge), f32)
            last = jnp.zeros((rows_v, LANES), f32)
            for n in range(tail):
                row = inv_tail[n : n + 1, :]
                more = more + rhs[:, edge + n : edge + n + 1] * row[:, :edge]
                value = jnp.sum(rhs * row, axis=1, keepdims=True)
                last = jnp.where(iota((rows_v, LANES), 1) == n, value, last)
            ends.append((more, last))
        if len(cases) % 2:
            high.append(jnp.zeros((rows_v, edge), f32))
            mid.append(jnp.zeros((rows_v, edge), f32))
        count = len(high) * rows_v
        high = jnp.concatenate(high, axis=0).astype(bf16)
        left = jnp.concatenate([high, jnp.concatenate(mid, axis=0).astype(bf16)], axis=0)
        both = jnp.dot(left, inv_high[...], preferred_element_type=f32)
        rest = jnp.dot(high, inv_mid[...], preferred_element_type=f32)
        final = jnp.dot(left, inv_last[...], preferred_element_type=f32)
        both = both[:count] + both[count:] + rest
        step = edge - main
        final = final[:count, :step] + final[count:, :step] + final[:count, step:]
        out = []
        for n, (more, last) in enumerate(ends):
            rows = slice(n * rows_v, (n + 1) * rows_v)
            out.append(jnp.concatenate(
                [both[rows] + more[:, :main], final[rows] + more[:, main:], last], axis=1
            ))
        return out

    def build_slots():
        column_of = []
        for h in range(blocks_v):
            rows = slot8[0, :, h * LANES : (h + 1) * LANES].astype(f32)
            turned[0, h * rows_v : (h + 1) * rows_v, :] = rows
        columns = jnp.transpose(turned[0]).astype(i32)
        for t in range(wide_tiles):
            q = iota((LANES, LANES), 1)
            brick = q // GROUP + t * (LANES // GROUP)
            inner = q % GROUP
            target = brick - 1 + inner // peer_cells
            target = jnp.where(target < 0, target + n_brick, target)
            target = jnp.where(target >= n_brick, target - n_brick, target)
            slot = jnp.where(inner < 3 * peer_cells, target * peer_cells + inner % peer_cells, -2)
            for b in range(bodies):
                for h in range(blocks_v):
                    at = h * rows_v + b * BODY_ROWS
                    column = jnp.broadcast_to(columns[:, at : at + 1], (LANES, LANES))
                    slot_hot[b, h * LANES : (h + 1) * LANES, t * LANES : (t + 1) * LANES] = jnp.where(
                        column == slot, 1.0, 0.0
                    ).astype(bf16)

    def build_deposit():
        for copy in cells_copies:
            copy.wait_recv()
        per_tile = LANES // GROUP
        for dg in range(3):
            for t in range(wide_tiles):
                start = t * per_tile * peer_cells
                source, offset = start // LANES, start % LANES
                index = offset + of_group * peer_cells + in_group % peer_cells
                side = in_group // peer_cells
                cell = jnp.zeros((8, LANES), i32)
                for db in range(3):
                    ref = cells_own if (dg, db) == (1, 1) else cells_near.at[dg, db]
                    row = ref[0:1, source * LANES : (source + 1) * LANES]
                    moved = take(jnp.broadcast_to(row, (8, LANES)), index)
                    cell = jnp.where(side == db, moved, cell)
                line = cell >> 7
                x = jnp.zeros((8, LANES), i32)
                for edge_x in range(1, cx):
                    x = x + jnp.where(line >= edge_x * cy, 1, 0)
                y = line - x * cy + cy * (side - 1) + RING
                inside = (y >= 0) & (y < long_y) & (side < 3)
                at = dg * wide_tiles + t
                row_id[dg, :, t * LANES : (t + 1) * LANES] = jnp.where(inside, x * long_y + y, -1)
                turned[1, at : at + 1, :] = (cell & (LANES - 1))[0:1, :].astype(f32)
        columns = jnp.transpose(turned[1]).astype(i32)
        for dg in range(3):
            for t in range(wide_tiles):
                at = dg * wide_tiles + t
                column = jnp.broadcast_to(columns[:, at : at + 1], (LANES, LANES))
                deposit[dg, t * LANES : (t + 1) * LANES, :] = jnp.where(
                    column == lane_square, 1.0, 0.0
                ).astype(bf16)

    def build_fluid():
        for copy in edge_copies + block_copies:
            copy.wait_recv()
        for i in range(DIRS):
            for dg in range(3):
                source = pop_ref if dg == 1 else blocks.at[0 if dg == 0 else 1]
                for x in range(cx):
                    at = (dg * cx + x) * long_y
                    fluid[i, at + RING : at + RING + cy, :] = source[i, x]
                    fluid[i, at + RING + cy : at + long_y, :] = edges_in[dg, 0, i, 2 * x : 2 * x + 2, :]
                    fluid[i, at : at + RING, :] = edges_in[dg, 1, i, 2 * x : 2 * x + 2, :]

    def send_force(predicted, shape, step):
        change = coupling_gain * (shape - predicted)
        left = jnp.concatenate(halves(change), axis=0).astype(bf16)
        total = None
        for b in range(bodies):
            got = jnp.dot(left, slot_hot[b], preferred_element_type=f32)
            got = got[:rows_v] + got[rows_v:]
            if b:
                got = pltpu.roll(got, rows_v - b * BODY_ROWS, 0)
            total = got if total is None else total + got
        per_tile = LANES // GROUP
        index = (sub8 % per_tile) * GROUP + in_group
        for base in range(0, n_brick, 8):
            message = jnp.zeros((8, LANES), f32)
            for c in range(3):
                for n in range(8 // per_tile):
                    t = base // per_tile + n
                    row = total[c : c + 1, t * LANES : (t + 1) * LANES]
                    moved = take(jnp.broadcast_to(row, (8, LANES)), index)
                    chosen = (of_group == c) & (sub8 // per_tile == n)
                    message = jnp.where(chosen, moved, message)
            for s in range(8):
                force_out[step, base + s] = message[s : s + 1, :]
        pltpu.make_async_copy(
            force_out.at[step, me], force_in.at[step, n_brick + me], force_recv.at[step]
        ).start()
        for dg, o in near:
            remote(
                force_out.at[step, brick_at(o)], force_in.at[step, (1 - dg) * n_brick + me],
                force_send.at[step], force_recv.at[step], dg, o,
            )

    def gather_force(step):
        all_bytes(force_in.at[step], force_recv.at[step])
        per_tile = LANES // GROUP
        index = jnp.minimum(sub8, 3) * GROUP + in_group
        for dg in range(3):
            parts = []
            for t in range(wide_tiles):
                table = jnp.zeros((8, LANES), f32)
                for n in range(per_tile):
                    row = force_in[step, dg * n_brick + t * per_tile + n]
                    moved = take(jnp.broadcast_to(row, (8, LANES)), index)
                    table = jnp.where(of_group == n, moved, table)
                parts.append(table)
            table = jnp.concatenate(parts, axis=1)
            ids = jnp.broadcast_to(row_id[dg, 0:1, :], (part, wide))
            chosen = ids == iota((part, wide), 0)
            left = []
            pieces = halves(table)
            for c in range(3):
                for piece in pieces:
                    row = jnp.broadcast_to(piece[c : c + 1, :], (part, wide))
                    left.append(jnp.where(chosen, row, 0.0))
            left = jnp.concatenate(left, axis=0).astype(bf16)
            got = jnp.dot(left, deposit[dg], preferred_element_type=f32)
            for c in range(3):
                field[c, dg * part : (dg + 1) * part, :] = (
                    got[2 * c * part : (2 * c + 1) * part] + got[(2 * c + 1) * part : (2 * c + 2) * part]
                )

    def nothing():
        pass

    def both_contacts(own, n, before_far):
        first_touch = contact(0, own, lower.at[n, 0], before_far)
        return [first_touch, contact(1, lower.at[n, 0], lower.at[n, 1], nothing)]

    def wait_start():
        for copy in start_copies + ghost_copies[:2]:
            copy.wait_recv()
        build_pairs(1, pairs_near.at[0])
        place_slots(1, slots_near.at[0])

    def wait_middle():
        build_slots()
        build_deposit()
        build_ghosts()
        for copy in middle_copies:
            copy.wait_recv()

    touches = both_contacts(shapes.at[0], 0, wait_start)
    all_bytes(flow_in.at[0], flow_recv.at[0])
    predicted_of[0] = shapes[0] + time_step * vertex_flow(0, 0)
    predicted_of[1] = lower[0, 0] + time_step * vertex_flow(0, 1)
    for n in range(ITERS // 2):
        if n:
            middle_copies = send_shapes(n)
            touches = both_contacts(shapes.at[2 * n], n, wait_middle)
        shapes[2 * n + 1], under[n] = relax([
            (shapes[2 * n], predicted_of[0], touches[0]), (lower[n, 0], predicted_of[1], touches[1])
        ])
        touch = contact(0, shapes.at[2 * n + 1], under.at[n], nothing)
        (shape,) = relax([(shapes[2 * n + 1], predicted_of[0], touch)])
        shapes[2 * n + 2] = shape
    predicted = predicted_of[0]
    send_force(predicted, shape, 0)
    near_copies = [
        remote(shapes.at[ITERS], shapes_near.at[e - 1], near_send.at[e - 1], near_recv.at[e - 1], 0, e)
        for e in range(1, depth + 1)
    ]
    build_fluid()
    gather_force(0)
    for q in range(3 * part // 8):
        rows = slice(8 * q, 8 * q + 8)
        after = collide([fluid[i, rows, :] for i in range(DIRS)], [field[c, rows, :] for c in range(3)])
        for i in range(DIRS):
            post[i, rows, :] = roll_z(after[i], i)
    for i in range(DIRS):
        step_x, step_y, _ = velocities[i]
        for x in range(cx + 2):
            at = (x + 1 - step_x) * long_y + 1 - step_y
            fluid_2[i, x * short_y : (x + 1) * short_y, :] = post[i, at : at + short_y, :]
    lines_own = [
        jnp.concatenate(
            [fluid_2[i, (x + 1) * short_y + 1 : (x + 1) * short_y + 1 + cy, :] for x in range(cx)], axis=0
        )
        for i in range(DIRS)
    ]
    density, momentum = moments(lines_own)
    inverse_density = 1.0 / density
    sample([m * inverse_density for m in momentum], 1)
    send_flow(1)

    for copy in near_copies:
        copy.wait_recv()
    level = [shapes.at[ITERS]] + [shapes_near.at[e - 1] for e in range(1, depth + 1)]
    touches = [contact(e, level[e], level[e + 1], nothing) for e in range(depth)]
    all_bytes(flow_in.at[1], flow_recv.at[1])
    for e in range(depth):
        predicted_of[e] = level[e][...] + time_step * vertex_flow(1, e)
    for sweep in range(ITERS):
        count = ITERS - sweep
        made = relax([(level[e][...], predicted_of[e], touches[e]) for e in range(count)])
        for e in range(count):
            ghosts[sweep, e] = made[e]
        level = [ghosts.at[sweep, e] for e in range(count)]
        touches = [contact(e, level[e], level[e + 1], nothing) for e in range(count - 1)]
    send_force(predicted_of[0], made[0], 1)

    outp_ref[...] = ghosts[ITERS - 1, 0]
    gather_force(1)
    for c in range(3):
        for x in range(cx + 2):
            at = (x + 1) * long_y + 1
            field_2[c, x * short_y : (x + 1) * short_y, :] = field[c, at : at + short_y, :]
    for q in range((cx + 2) * short_y // 8):
        rows = slice(8 * q, 8 * q + 8)
        after = collide([fluid_2[i, rows, :] for i in range(DIRS)], [field_2[c, rows, :] for c in range(3)])
        for i in range(DIRS):
            post_2[i, rows, :] = roll_z(after[i], i)
    for i in range(DIRS):
        step_x, step_y, _ = velocities[i]
        for x in range(cx):
            at = (x + 1 - step_x) * short_y + 1 - step_y
            outf_ref[i, x] = post_2[i, at : at + cy, :]

    for copy in start_copies + middle_copies:
        copy.wait_send()
    for copy in cells_copies + edge_copies + block_copies + ghost_copies + near_copies:
        copy.wait_send()
    for step in range(STEPS):
        all_bytes(flow_out.at[step, pl.ds(0, n_brick - 1)], flow_send.at[step])
        all_bytes(force_in.at[step, pl.ds(0, 3 * n_brick - 1)], force_send.at[step])


def finish_kernel(fluid_ref, rows_ref, outf_ref, outp_ref):
    outf_ref[...] = fluid_ref[...]
    bodies, verts = outp_ref.shape[1:]
    for b in range(bodies):
        for c in range(3):
            r = b * BODY_ROWS + c
            outp_ref[c, b : b + 1, :] = rows_ref[r : r + 1, 0:verts]


def on_device(
    populations, positions, rest_shape, inverse, sample_cells, vertex_slots, pair_own, pair_far
):
    n_brick = lax.axis_size("brick")
    n_group = lax.axis_size("group")
    slot_count = sample_cells.shape[1]
    bodies, verts = positions.shape[1:]
    width = up(verts, LANES)
    rows = bodies * BODY_ROWS
    dirs, cx, cy, lanes = populations.shape
    tiles = pair_own.shape[1] // LANES
    wide = n_brick * GROUP
    long_rows = 3 * cx * (cy + 2 * RING)
    short_rows = (cx + 2) * (cy + 2)
    blocks_v = width // LANES
    edge = verts // LANES * LANES
    main = edge // (2 * LANES) * (2 * LANES)
    f32, bf16, i32 = jnp.float32, jnp.bfloat16, jnp.int32
    vmem = pltpu.VMEM
    dma = pltpu.SemaphoreType.DMA
    in_vmem = pl.BlockSpec(memory_space=pltpu.VMEM)
    fluid, shape_rows = pl.pallas_call(
        functools.partial(step_kernel, (n_brick, n_group, verts, bodies, slot_count)),
        out_shape=(vmem(populations.shape, f32), vmem((rows, width), f32)),
        in_specs=[pl.BlockSpec(memory_space=pltpu.HBM)] * 8,
        out_specs=(in_vmem, in_vmem),
        scratch_shapes=[
            vmem(populations.shape, f32),
            vmem(positions.shape, f32),
            vmem(rest_shape.shape, f32),
            vmem(sample_cells.shape, i32),
            vmem(vertex_slots.shape, i32),
            vmem((2, tiles, LANES), i32),
            vmem((verts, verts), f32),
            vmem((up(max(verts - edge, 1), 8), width), f32),
            vmem((edge, main), bf16),
            vmem((edge, main), bf16),
            vmem((edge, 2 * (edge - main)), bf16),
            vmem((ITERS, 4, tiles, LANES), i32),
            vmem((ITERS, tiles * LANES, LANES), bf16),
            vmem((ITERS, tiles, blocks_v * rows, LANES), bf16),
            vmem((ITERS, 2 * blocks_v * rows, tiles * LANES), bf16),
            vmem((ITERS, rows * tiles, LANES), f32),
            vmem((bodies, width, wide), bf16),
            vmem((3, wide, LANES), bf16),
            vmem((3, 8, wide), i32),
            vmem((ITERS, LANES, LANES), f32),
            vmem((ITERS + 1, rows, width), f32),
            vmem((ITERS // 2, 2, rows, width), f32),
            vmem((ITERS // 2, rows, width), f32),
            vmem((ITERS, rows, width), f32),
            vmem((ITERS - 1, 2, tiles, LANES), i32),
            vmem((ITERS - 1,) + vertex_slots.shape, i32),
            vmem((ITERS, ITERS, rows, width), f32),
            vmem((ITERS, rows, width), f32),
            vmem((rows, width), f32),
            vmem((ITERS, rows, width), i32),
            vmem((ITERS, 1, up(bodies * verts + width, LANES)), i32),
            vmem((1, up(slot_count, LANES)), i32),
            vmem((3, 3, 1, up(slot_count, LANES)), i32),
            vmem((STEPS, n_brick, 1, LANES), f32),
            vmem((STEPS, n_brick, 1, LANES), f32),
            vmem((STEPS, n_brick, 1, LANES), f32),
            vmem((STEPS, 3 * n_brick, 1, LANES), f32),
            vmem((2,) + populations.shape, f32),
            vmem((2, dirs, 2 * cx, LANES), f32),
            vmem((3, 2, dirs, 2 * cx, LANES), f32),
            vmem((dirs, long_rows, LANES), f32),
            vmem((dirs, long_rows, LANES), f32),
            vmem((dirs, short_rows, LANES), f32),
            vmem((dirs, short_rows, LANES), f32),
            vmem((3, long_rows, LANES), f32),
            vmem((3, short_rows, LANES), f32),
            dma((8,)),
            pltpu.SemaphoreType.REGULAR,
            dma((ITERS // 2, 2)),
            dma((ITERS // 2, 2)),
            dma((ITERS,)),
            dma((ITERS,)),
            dma((ITERS - 1,)),
            dma((ITERS - 1,)),
            dma((ITERS - 1,)),
            dma((ITERS - 1,)),
            dma((STEPS,)),
            dma((STEPS,)),
            dma((STEPS,)),
            dma((STEPS,)),
            dma((8,)),
            dma((8,)),
            dma((3, 2)),
            dma((3, 2)),
            dma((2,)),
            dma((2,)),
        ],
        compiler_params=pltpu.CompilerParams(
            collective_id=0, has_side_effects=True, vmem_limit_bytes=48 * 1024 * 1024
        ),
    )(*[
        pltpu.with_memory_space_constraint(value, pltpu.HBM)
        for value in (
            populations, positions, rest_shape, inverse, sample_cells, vertex_slots,
            pair_own.reshape(tiles, LANES), pair_far.reshape(tiles, LANES),
        )
    ])
    return pl.pallas_call(
        finish_kernel,
        out_shape=(
            jax.ShapeDtypeStruct(populations.shape, f32),
            jax.ShapeDtypeStruct(positions.shape, f32),
        ),
        in_specs=[in_vmem, in_vmem],
        out_specs=(in_vmem, in_vmem),
        compiler_params=pltpu.CompilerParams(vmem_limit_bytes=8 * 1024 * 1024),
    )(fluid, shape_rows)


def solution(mesh):
    placed = (
        P(None, "group", "brick", None),
        P(None, ("group", "brick"), None),
        P(),
        P(),
        P(("group", "brick"), None),
        P(("group", "brick"), None),
        P(("group", "brick"), None),
        P(("group", "brick"), None),
    )
    return jax.shard_map(
        on_device,
        mesh=mesh,
        in_specs=placed,
        out_specs=(P(None, "group", "brick", None), P(None, ("group", "brick"), None)),
        check_vma=False,
    )
```

```python
import functools

import jax
import jax.numpy as jnp
from jax import lax
from jax.experimental import pallas as pl
from jax.experimental.pallas import tpu as pltpu
from jax.sharding import PartitionSpec as P

ITERS = 4
STEPS = 2

velocities = [
    (0, 0, 0),
    (0, 0, 1),
    (0, 0, -1),
    (1, 0, 0),
    (-1, 0, 0),
    (0, 1, 0),
    (0, -1, 0),
    (1, 1, 0),
    (-1, -1, 0),
    (1, -1, 0),
    (-1, 1, 0),
    (1, 0, 1),
    (-1, 0, -1),
    (1, 0, -1),
    (-1, 0, 1),
    (0, 1, 1),
    (0, -1, -1),
    (0, 1, -1),
    (0, -1, 1),
]
weights_table = [1.0 / 3.0] + [1.0 / 18.0] * 6 + [1.0 / 36.0] * 12
DIRS = len(velocities)
relax_time = 0.8
contact_gain = 0.5
contact_range = 6.0
coupling_gain = 0.05
mass_weight = 1.0
shape_weight = 1.0
time_step = 1.0

LANES = 128
BODY_ROWS = 4
GROUP = 32
RING = 2
MESH = pl.DeviceIdType.MESH


def up(value, unit):
    return -(-value // unit) * unit


def take(rows, index):
    return jnp.take_along_axis(rows, index, axis=1, mode="promise_in_bounds")


def halves(value):
    high = value.astype(jnp.bfloat16).astype(jnp.float32)
    return high, value - high


def signed_sum(terms, axis):
    total = None
    for p in range(1, DIRS, 2):
        sign = velocities[p][axis]
        if sign == 0:
            continue
        if total is None:
            assert sign > 0
            total = terms[p]
        else:
            total = total + terms[p] if sign > 0 else total - terms[p]
    return total


def moments(rows):
    density = functools.reduce(lambda a, b: a + b, rows)
    opposite = {p: rows[p] - rows[p + 1] for p in range(1, DIRS, 2)}
    return density, [signed_sum(opposite, axis) for axis in range(3)]


def dot_c(vector, p):
    total = None
    for axis in range(3):
        sign = velocities[p][axis]
        if sign == 0:
            continue
        if total is None:
            total = vector[axis] if sign > 0 else -vector[axis]
        else:
            total = total + vector[axis] if sign > 0 else total - vector[axis]
    return total


def collide(rows, force):
    density, momentum = moments(rows)
    inverse_density = 1.0 / density
    veloc = [(momentum[a] + 0.5 * force[a]) * inverse_density for a in range(3)]
    square = veloc[0] * veloc[0] + veloc[1] * veloc[1] + veloc[2] * veloc[2]
    keep, gain = 1.0 - 1.0 / relax_time, 1.0 / relax_time
    base = 1.0 - 1.5 * square
    scaled = [density * (gain * w) for w in (1.0 / 3.0, 1.0 / 18.0, 1.0 / 36.0)]
    out = [None] * DIRS
    out[0] = keep * rows[0] + scaled[0] * base
    for p in range(1, DIRS, 2):
        weight = weights_table[p]
        rho = scaled[1] if p < 7 else scaled[2]
        along = dot_c(veloc, p)
        even = rho * (base + 4.5 * (along * along))
        odd = rho * (3.0 * along) + (3.0 * weight) * dot_c(force, p)
        out[p] = keep * rows[p] + (even + odd)
        out[p + 1] = keep * rows[p + 1] + (even - odd)
    return out


def far_dirs(sign):
    known = [i for i in range(DIRS) if velocities[i][0] == sign]
    return known + [velocities.index((-sign, 0, 0)), velocities.index((0, 1, 0)), velocities.index((0, 0, 1)), 0]


def far_rows(rows, sign):
    density, momentum = moments(rows)
    known = far_dirs(sign)[:5]
    ahead = functools.reduce(lambda a, b: a + b, [rows[i] for i in known])
    back = ahead - momentum[0] if sign > 0 else ahead + momentum[0]
    at = velocities.index
    side = momentum[1] - (rows[at((sign, 1, 0))] - rows[at((sign, -1, 0))])
    along = momentum[2] - (rows[at((sign, 0, 1))] - rows[at((sign, 0, -1))])
    return [rows[i] for i in known] + [back, side, along, density - ahead - back - side - along]


def roll_z(value, index):
    step = velocities[index][2]
    if step == 0:
        return value
    return pltpu.roll(value, step % LANES, 1)


def step_kernel(
    sizes, pop_hbm, pos_hbm, rest_hbm, inv_hbm, cells_hbm, slots_hbm, own_hbm, far_hbm,
    outf_ref, outp_ref,
    pop_ref, pos_ref, rest_in, cells_ref, slots_ref, pairs,
    inv_raw, inv_tail, inv_high, inv_mid, inv_last, places, hot, mask, lhs, spread, slot_hot, deposit, row_id, turned,
    shapes, lower, under, shapes_near, pairs_near, slots_near, ghosts, predicted_of,
    rest8, slot8, slot_flat, cells_own, cells_near,
    flow_out, flow_in, force_out, force_in, far_out, far_in, corner_out, corner_in, edges_out, edges_in, fluid, post, fluid_own,
    field, field_near,
    in_sem, ready, ring_send, ring_recv, near_send, near_recv, pairs_send, pairs_recv, slots_send, slots_recv, flow_send, flow_recv, force_send, force_recv,
    cells_send, cells_recv, edge_send, edge_recv, far_send, far_recv, corner_send, corner_recv,
):
    n_brick, n_group, verts, bodies, slot_count = sizes
    me = lax.axis_index("brick")
    group = lax.axis_index("group")
    cx, cy = pop_ref.shape[1:3]
    width = shapes.shape[2]
    blocks_v = width // LANES
    rows_v = bodies * BODY_ROWS
    tiles = pairs.shape[1]
    depth = ITERS
    peer_cells = slot_count // n_brick
    wide = n_brick * GROUP
    wide_tiles = wide // LANES
    slot_tiles = cells_own.shape[1] // LANES
    long_y = cy + 2 * RING
    short_y = cy + 2
    part = cx * long_y
    f32, bf16, i32 = jnp.float32, jnp.bfloat16, jnp.int32

    def brick_at(offset):
        return lax.rem(me + (offset + n_brick), n_brick)

    def group_at(offset):
        return lax.rem(group + (offset + n_group), n_group)

    def iota(shape, axis):
        return lax.broadcasted_iota(i32, shape, axis)

    by_reach = sorted(range(n_brick), key=lambda o: -min(o, n_brick - o))
    near = [(dg, o) for dg in (1, -1, 0) for o in by_reach if (dg, o) != (0, 0)]
    first = [(0, o) for o in range(1, n_brick)] + [(1, 0), (-1, 0)]
    barrier = pltpu.get_barrier_semaphore()
    for dg, o in first:
        pl.semaphore_signal(barrier, inc=1, device_id=(group_at(dg), brick_at(o)), device_id_type=MESH)
    loads = [
        pltpu.make_async_copy(source, target, in_sem.at[n])
        for n, (source, target) in enumerate([
            (pop_hbm, pop_ref), (cells_hbm, cells_ref), (pos_hbm, pos_ref), (rest_hbm, rest_in),
            (own_hbm, pairs.at[0]), (far_hbm, pairs.at[1]), (slots_hbm, slots_ref), (inv_hbm, inv_raw),
        ])
    ]
    for load in loads:
        load.start()
    inv_copy = loads.pop()
    for load in loads:
        load.wait()

    def remote(source, target, send, recv, dg, o):
        copy = pltpu.make_async_remote_copy(
            src_ref=source, dst_ref=target, send_sem=send, recv_sem=recv,
            device_id=(group_at(dg), brick_at(o)), device_id_type=MESH,
        )
        copy.start()
        return copy

    def all_bytes(ref, sem):
        pltpu.make_async_copy(ref, ref, sem).wait()

    shapes[0] = jnp.zeros((rows_v, width), f32)
    rest8[...] = jnp.zeros((rows_v, width), f32)
    for b in range(bodies):
        for c in range(3):
            r = b * BODY_ROWS + c
            shapes[0, r : r + 1, 0:verts] = pos_ref[c, b : b + 1, :]
            rest8[r : r + 1, 0:verts] = rest_in[c : c + 1, :]
    cells_own[...] = jnp.zeros(cells_own.shape, i32)
    cells_own[:, 0:slot_count] = cells_ref[...]
    lane8 = iota((8, LANES), 1)
    sub8 = iota((8, LANES), 0)
    in_group = lane8 % GROUP
    of_group = lane8 // GROUP

    def sample(flow, step):
        lines = cx * cy
        got = []
        for t in range(slot_tiles):
            cell = cells_own[0:1, t * LANES : (t + 1) * LANES]
            at = jnp.broadcast_to(cell & (LANES - 1), (lines, LANES))
            chosen = jnp.broadcast_to(cell >> 7, (lines, LANES)) == iota((lines, LANES), 0)
            got.append([
                jnp.sum(jnp.where(chosen, take(flow[c], at), 0.0), axis=0, keepdims=True) for c in range(3)
            ])
        for base in range(0, n_brick, 8):
            owner = base + sub8 - in_group // peer_cells
            owner = jnp.where(owner < 0, owner + n_brick, owner)
            slot = owner * peer_cells + in_group % peer_cells
            touched = {(base + n) % n_brick * peer_cells // LANES for n in range(1 - depth, 8)}
            message = jnp.zeros((8, LANES), f32)
            for c in range(3):
                for t in sorted(touched):
                    moved = take(jnp.broadcast_to(got[t][c], (8, LANES)), slot & (LANES - 1))
                    message = jnp.where((of_group == c) & (slot >> 7 == t), moved, message)
            for s in range(8):
                flow_out[step, base + s] = message[s : s + 1, :]

    def send_flow(step):
        pltpu.make_async_copy(flow_out.at[step, me], flow_in.at[step, me], flow_recv.at[step]).start()
        for o in by_reach[:-1]:
            remote(
                flow_out.at[step, brick_at(o)], flow_in.at[step, me],
                flow_send.at[step], flow_recv.at[step], 0, o,
            )

    def send_shapes(n):
        return [
            remote(
                shapes.at[2 * n], lower.at[n, e - 1], ring_send.at[n, e - 1], ring_recv.at[n, e - 1], 0, e
            )
            for e in (1, 2)
        ]

    def send_pairs(e):
        return remote(pairs, pairs_near.at[e - 1], pairs_send.at[e - 1], pairs_recv.at[e - 1], 0, e)

    def send_slots(e):
        return remote(slots_ref, slots_near.at[e - 1], slots_send.at[e - 1], slots_recv.at[e - 1], 0, e)

    lines_own = [
        jnp.concatenate([pop_ref[i, x] for x in range(cx)], axis=0) for i in range(DIRS)
    ]
    density, momentum = moments(lines_own)
    inverse_density = 1.0 / density
    sample([m * inverse_density for m in momentum], 0)

    pl.semaphore_wait(barrier, len(first))
    for dg in (1, -1):
        pl.semaphore_signal(ready, inc=1, device_id=(group_at(dg), brick_at(0)), device_id_type=MESH)
    send_flow(0)
    start_copies = send_shapes(0)
    ghost_copies = [send_pairs(1), send_slots(1)]
    def fill_ring(step, lines):
        for n, sign in enumerate((1, -1)):
            close = cx - 1 if sign > 0 else 0
            for m, value in enumerate(far_rows(lines, sign)):
                far_out[step, n, m] = value[close * cy : (close + 1) * cy]
                for side, y in enumerate((0, cy - 1)):
                    corner_out[step, n, side, m] = value[close * cy + y : close * cy + y + 1]
        for i in range(DIRS):
            for x in range(cx):
                for side, y in enumerate((0, cy - 1)):
                    edges_out[step, side, i, x] = lines[i][x * cy + y : x * cy + y + 1]

    def send_sides(step):
        return [
            remote(
                far_out.at[step, n], far_in.at[step, n], far_send.at[step, n], far_recv.at[step, n], dg, 0
            )
            for n, dg in enumerate((1, -1))
        ] + [
            remote(
                edges_out.at[step, side], edges_in.at[step, side],
                edge_send.at[step, side], edge_recv.at[step, side], 0, 2 * side - 1,
            )
            for side in (0, 1)
        ]

    def send_corners(step):
        return [
            remote(
                corner_out.at[step, n, side], corner_in.at[step, n, side],
                corner_send.at[step, 2 * n + side], corner_recv.at[step, 2 * n + side], dg, 2 * side - 1,
            )
            for n, dg in enumerate((1, -1))
            for side in (0, 1)
        ]

    lines_own = [
        jnp.concatenate([pop_ref[i, x] for x in range(cx)], axis=0) for i in range(DIRS)
    ]
    fill_ring(0, lines_own)
    rim_copies = send_sides(0)

    def place(index):
        body = jnp.zeros(index.shape, i32)
        for b in range(1, bodies):
            body = body + jnp.where(index >= b * verts, 1, 0)
        vertex = index - body * verts
        return vertex & (LANES - 1), vertex >> 7, body

    lane_square = iota((LANES, LANES), 1)

    def build_pairs(e, ref):
        own_lane, own_block, own_body = place(ref[0])
        far_lane, far_block, far_body = place(ref[1])
        places[e, 0] = own_lane
        places[e, 1] = own_body * blocks_v + own_block
        places[e, 2] = far_lane
        places[e, 3] = far_body * blocks_v + far_block
        turned[e, 0:tiles, :] = own_lane.astype(f32)
        turned[e, tiles:LANES, :] = jnp.zeros((LANES - tiles, LANES), f32)
        columns = jnp.transpose(turned[e]).astype(i32)
        for t in range(tiles):
            column = jnp.broadcast_to(columns[:, t : t + 1], (LANES, LANES))
            hot[e, t * LANES : (t + 1) * LANES, :] = jnp.where(column == lane_square, 1.0, 0.0).astype(bf16)
            chosen = jnp.broadcast_to(own_block[t : t + 1, :], (blocks_v * rows_v, LANES))
            mask[e, t] = jnp.where(
                chosen == iota((blocks_v * rows_v, LANES), 0) // rows_v, 1.0, 0.0
            ).astype(bf16)

    def place_slots(e, ref):
        slot_flat[e, :, 0 : bodies * verts] = ref[...]
        total = slot_flat.shape[2]
        flat = jnp.broadcast_to(slot_flat[e], (8, total))
        picked = flat[:, :width]
        row_body = iota((rows_v, width), 0) // BODY_ROWS
        for b in range(1, bodies):
            moved = pltpu.roll(flat, total - b * verts, 1)[:, :width]
            picked = jnp.where(row_body == b, moved, picked)
        slot8[e] = jnp.where(iota((rows_v, width), 1) < verts, picked, -1)

    slot_flat[...] = jnp.zeros(slot_flat.shape, i32)
    spread[...] = jnp.zeros(spread.shape, f32)
    build_pairs(0, pairs)
    place_slots(0, slots_ref)

    def build_ghosts():
        for copy in ghost_copies[2:]:
            copy.wait_recv()
        for e in range(2, depth):
            build_pairs(e, pairs_near.at[e - 1])
            place_slots(e, slots_near.at[e - 1])

    inv_copy.wait()
    chunk = 32
    edge = verts // LANES * LANES
    tail = verts - edge
    main = inv_high.shape[1]
    inv_tail[...] = jnp.zeros(inv_tail.shape, f32)
    inv_tail[0:tail, 0:verts] = inv_raw[edge:verts, :]

    def split(n, _):
        at = pl.multiple_of(n * chunk, chunk)
        high, mid = halves(inv_raw[pl.ds(at, chunk), 0:edge])
        high = high.astype(bf16)
        mid = mid.astype(bf16)
        inv_high[pl.ds(at, chunk), :] = high[:, :main]
        inv_mid[pl.ds(at, chunk), :] = mid[:, :main]
        inv_last[pl.ds(at, chunk), 0 : edge - main] = high[:, main:]
        inv_last[pl.ds(at, chunk), edge - main : 2 * (edge - main)] = mid[:, main:]
        return 0

    lax.fori_loop(0, edge // chunk, split, 0)

    def pick(ref, lane, ident):
        total = [jnp.zeros((tiles, LANES), f32)] * 3
        for b in range(bodies):
            for h in range(blocks_v):
                chosen = ident == b * blocks_v + h
                for c in range(3):
                    r = b * BODY_ROWS + c
                    row = ref[r : r + 1, h * LANES : (h + 1) * LANES]
                    got = take(jnp.broadcast_to(row, (tiles, LANES)), lane)
                    total[c] = jnp.where(chosen, got, total[c])
        return total

    def contact(e, shape_of, lower_of, before_far):
        own_id = places[e, 1]
        own = pick(shape_of, places[e, 0], own_id)
        before_far()
        far = pick(lower_of, places[e, 2], places[e, 3])
        diff = [a - b for a, b in zip(own, far)]
        square = diff[0] * diff[0] + diff[1] * diff[1] + diff[2] * diff[2]
        scale = contact_gain * jnp.exp(-square / contact_range)
        for b in range(bodies):
            inside = (own_id >= b * blocks_v) & (own_id < (b + 1) * blocks_v)
            for c in range(3):
                r = b * BODY_ROWS + c
                spread[e, r * tiles : (r + 1) * tiles, :] = jnp.where(inside, scale * diff[c], 0.0)
        half = blocks_v * rows_v
        for t in range(tiles):
            push = spread[e, pl.ds(t, rows_v, stride=tiles), :]
            for n, piece in enumerate(halves(push)):
                pair = jnp.concatenate([piece, piece], axis=0).astype(bf16)
                lhs[e, n * half : (n + 1) * half, t * LANES : (t + 1) * LANES] = (
                    jnp.concatenate([pair] * (blocks_v // 2), axis=0) * mask[e, t]
                )
        middle = tiles // 2 * LANES
        added = jnp.dot(lhs[e, :, :middle], hot[e, :middle], preferred_element_type=f32)
        added = added + jnp.dot(lhs[e, :, middle:], hot[e, middle:], preferred_element_type=f32)
        added = added[:half] + added[half:]
        return jnp.concatenate([added[h * rows_v : (h + 1) * rows_v] for h in range(blocks_v)], axis=1)

    def received(step, e):
        out = []
        per_tile = LANES // peer_cells
        for t in range(slot_tiles):
            index = (sub8 % BODY_ROWS) * GROUP + e * peer_cells + lane8 % peer_cells
            table = jnp.zeros((8, LANES), f32)
            for s in range(t * per_tile, min((t + 1) * per_tile, n_brick)):
                moved = take(jnp.broadcast_to(flow_in[step, s], (8, LANES)), index)
                table = jnp.where(lane8 // peer_cells == s % per_tile, moved, table)
            out.append(table)
        return out

    def vertex_flow(step, e):
        tables = received(step, e)
        parts = []
        for h in range(blocks_v):
            slot = jnp.maximum(slot8[e, :, h * LANES : (h + 1) * LANES], 0)
            got = take(tables[0], slot & (LANES - 1))
            for t in range(1, slot_tiles):
                got = jnp.where(slot >> 7 == t, take(tables[t], slot & (LANES - 1)), got)
            parts.append(got)
        return jnp.concatenate(parts, axis=1)

    def relax(cases):
        high, mid, ends = [], [], []
        for shape, predicted, touch in cases:
            centroid = jnp.sum(shape, axis=1, keepdims=True) * (1.0 / verts)
            rhs = mass_weight * predicted + shape_weight * (centroid + rest8[...]) + touch
            a, b = halves(rhs[:, :edge])
            high.append(a)
            mid.append(b)
            more = jnp.zeros((rows_v, edge), f32)
            last = jnp.zeros((rows_v, LANES), f32)
            for n in range(tail):
                row = inv_tail[n : n + 1, :]
                more = more + rhs[:, edge + n : edge + n + 1] * row[:, :edge]
                value = jnp.sum(rhs * row, axis=1, keepdims=True)
                last = jnp.where(iota((rows_v, LANES), 1) == n, value, last)
            ends.append((more, last))
        if len(cases) % 2:
            high.append(jnp.zeros((rows_v, edge), f32))
            mid.append(jnp.zeros((rows_v, edge), f32))
        count = len(high) * rows_v
        high = jnp.concatenate(high, axis=0).astype(bf16)
        left = jnp.concatenate([high, jnp.concatenate(mid, axis=0).astype(bf16)], axis=0)
        both = jnp.dot(left, inv_high[...], preferred_element_type=f32)
        rest = jnp.dot(high, inv_mid[...], preferred_element_type=f32)
        final = jnp.dot(left, inv_last[...], preferred_element_type=f32)
        both = both[:count] + both[count:] + rest
        step = edge - main
        final = final[:count, :step] + final[count:, :step] + final[:count, step:]
        out = []
        for n, (more, last) in enumerate(ends):
            rows = slice(n * rows_v, (n + 1) * rows_v)
            out.append(jnp.concatenate(
                [both[rows] + more[:, :main], final[rows] + more[:, main:], last], axis=1
            ))
        return out

    def build_slots():
        column_of = []
        for h in range(blocks_v):
            rows = slot8[0, :, h * LANES : (h + 1) * LANES].astype(f32)
            turned[0, h * rows_v : (h + 1) * rows_v, :] = rows
        columns = jnp.transpose(turned[0]).astype(i32)
        for t in range(wide_tiles):
            q = iota((LANES, LANES), 1)
            brick = q // GROUP + t * (LANES // GROUP)
            inner = q % GROUP
            target = brick - 1 + inner // peer_cells
            target = jnp.where(target < 0, target + n_brick, target)
            target = jnp.where(target >= n_brick, target - n_brick, target)
            slot = jnp.where(inner < 3 * peer_cells, target * peer_cells + inner % peer_cells, -2)
            for b in range(bodies):
                for h in range(blocks_v):
                    at = h * rows_v + b * BODY_ROWS
                    column = jnp.broadcast_to(columns[:, at : at + 1], (LANES, LANES))
                    slot_hot[b, h * LANES : (h + 1) * LANES, t * LANES : (t + 1) * LANES] = jnp.where(
                        column == slot, 1.0, 0.0
                    ).astype(bf16)

    def build_deposit():
        for copy in cells_copies:
            copy.wait_recv()
        per_tile = LANES // GROUP
        for dg in range(3):
            for t in range(wide_tiles):
                start = t * per_tile * peer_cells
                source, offset = start // LANES, start % LANES
                index = offset + of_group * peer_cells + in_group % peer_cells
                side = in_group // peer_cells
                cell = jnp.zeros((8, LANES), i32)
                for db in range(3):
                    ref = cells_own if (dg, db) == (1, 1) else cells_near.at[dg, db]
                    row = ref[0:1, source * LANES : (source + 1) * LANES]
                    moved = take(jnp.broadcast_to(row, (8, LANES)), index)
                    cell = jnp.where(side == db, moved, cell)
                line = cell >> 7
                x = jnp.zeros((8, LANES), i32)
                for edge_x in range(1, cx):
                    x = x + jnp.where(line >= edge_x * cy, 1, 0)
                y = line - x * cy + cy * (side - 1) + RING
                inside = (y >= 0) & (y < long_y) & (side < 3)
                at = dg * wide_tiles + t
                row_id[dg, :, t * LANES : (t + 1) * LANES] = jnp.where(inside, x * long_y + y, -1)
                turned[1, at : at + 1, :] = (cell & (LANES - 1))[0:1, :].astype(f32)
        columns = jnp.transpose(turned[1]).astype(i32)
        for dg in range(3):
            for t in range(wide_tiles):
                at = dg * wide_tiles + t
                column = jnp.broadcast_to(columns[:, at : at + 1], (LANES, LANES))
                deposit[dg, t * LANES : (t + 1) * LANES, :] = jnp.where(
                    column == lane_square, 1.0, 0.0
                ).astype(bf16)

    def build_fluid(step, own, copies):
        for copy in copies:
            copy.wait_recv()

        def put(i, plane, middle, lower_end, upper_end):
            at = plane * short_y
            fluid[i, at + 1 : at + 1 + cy, :] = middle
            fluid[i, at : at + 1, :] = lower_end
            fluid[i, at + 1 + cy : at + short_y, :] = upper_end

        for i in range(DIRS):
            for x in range(cx):
                put(i, x + 1, own[i, x], edges_in[step, 1, i, x], edges_in[step, 0, i, x])
            for n, (plane, sign) in enumerate(((0, 1), (cx + 1, -1))):
                kept = far_dirs(sign)
                if i in kept:
                    m = kept.index(i)
                    put(i, plane, far_in[step, n, m], corner_in[step, n, 1, m], corner_in[step, n, 0, m])
                else:
                    fluid[i, plane * short_y : (plane + 1) * short_y, :] = jnp.zeros((short_y, LANES), f32)

    def advance(target):
        for c in range(3):
            for x in range(cx + 2):
                at = (x + 1) * long_y + 1
                field_near[c, x * short_y : (x + 1) * short_y, :] = field[c, at : at + short_y, :]
        for q in range((cx + 2) * short_y // 8):
            rows = slice(8 * q, 8 * q + 8)
            after = collide(
                [fluid[i, rows, :] for i in range(DIRS)], [field_near[c, rows, :] for c in range(3)]
            )
            for i in range(DIRS):
                post[i, rows, :] = roll_z(after[i], i)
        for i in range(DIRS):
            step_x, step_y, _ = velocities[i]
            for x in range(cx):
                at = (x + 1 - step_x) * short_y + 1 - step_y
                target[i, x] = post[i, at : at + cy, :]

    def send_force(predicted, shape, step):
        change = coupling_gain * (shape - predicted)
        left = jnp.concatenate(halves(change), axis=0).astype(bf16)
        total = None
        for b in range(bodies):
            got = jnp.dot(left, slot_hot[b], preferred_element_type=f32)
            got = got[:rows_v] + got[rows_v:]
            if b:
                got = pltpu.roll(got, rows_v - b * BODY_ROWS, 0)
            total = got if total is None else total + got
        per_tile = LANES // GROUP
        index = (sub8 % per_tile) * GROUP + in_group
        for base in range(0, n_brick, 8):
            message = jnp.zeros((8, LANES), f32)
            for c in range(3):
                for n in range(8 // per_tile):
                    t = base // per_tile + n
                    row = total[c : c + 1, t * LANES : (t + 1) * LANES]
                    moved = take(jnp.broadcast_to(row, (8, LANES)), index)
                    chosen = (of_group == c) & (sub8 // per_tile == n)
                    message = jnp.where(chosen, moved, message)
            for s in range(8):
                force_out[step, base + s] = message[s : s + 1, :]
        pltpu.make_async_copy(
            force_out.at[step, me], force_in.at[step, n_brick + me], force_recv.at[step]
        ).start()
        for dg, o in near:
            remote(
                force_out.at[step, brick_at(o)], force_in.at[step, (1 - dg) * n_brick + me],
                force_send.at[step], force_recv.at[step], dg, o,
            )

    def gather_force(step):
        all_bytes(force_in.at[step], force_recv.at[step])
        per_tile = LANES // GROUP
        index = jnp.minimum(sub8, 3) * GROUP + in_group
        for dg in range(3):
            parts = []
            for t in range(wide_tiles):
                table = jnp.zeros((8, LANES), f32)
                for n in range(per_tile):
                    row = force_in[step, dg * n_brick + t * per_tile + n]
                    moved = take(jnp.broadcast_to(row, (8, LANES)), index)
                    table = jnp.where(of_group == n, moved, table)
                parts.append(table)
            table = jnp.concatenate(parts, axis=1)
            ids = jnp.broadcast_to(row_id[dg, 0:1, :], (part, wide))
            chosen = ids == iota((part, wide), 0)
            left = []
            pieces = halves(table)
            for c in range(3):
                for piece in pieces:
                    row = jnp.broadcast_to(piece[c : c + 1, :], (part, wide))
                    left.append(jnp.where(chosen, row, 0.0))
            left = jnp.concatenate(left, axis=0).astype(bf16)
            got = jnp.dot(left, deposit[dg], preferred_element_type=f32)
            for c in range(3):
                field[c, dg * part : (dg + 1) * part, :] = (
                    got[2 * c * part : (2 * c + 1) * part] + got[(2 * c + 1) * part : (2 * c + 2) * part]
                )

    def nothing():
        pass

    def both_contacts(own, n, before_far, between):
        first_touch = contact(0, own, lower.at[n, 0], before_far)
        between()
        return [first_touch, contact(1, lower.at[n, 0], lower.at[n, 1], nothing)]

    def wait_start():
        start_copies[0].wait_recv()

    def wait_under():
        for copy in ghost_copies[:2]:
            copy.wait_recv()
        build_pairs(1, pairs_near.at[0])
        place_slots(1, slots_near.at[0])
        start_copies[1].wait_recv()

    def wait_middle():
        build_slots()
        for copy in middle_copies:
            copy.wait_recv()

    touches = both_contacts(shapes.at[0], 0, wait_start, wait_under)
    pl.semaphore_wait(ready, 2)
    cells_copies = []
    for n, (dg, db) in enumerate([(a, b) for a in (-1, 0, 1) for b in (-1, 0, 1) if (a, b) != (0, 0)]):
        cells_copies.append(remote(
            cells_own, cells_near.at[1 - dg, 1 - db], cells_send.at[n], cells_recv.at[n], dg, db
        ))
    rim_copies += send_corners(0)
    all_bytes(flow_in.at[0], flow_recv.at[0])
    predicted_of[0] = shapes[0] + time_step * vertex_flow(0, 0)
    predicted_of[1] = lower[0, 0] + time_step * vertex_flow(0, 1)
    for n in range(ITERS // 2):
        if n:
            middle_copies = send_shapes(n)
            for e in range(2, depth):
                ghost_copies.extend([send_pairs(e), send_slots(e)])
            touches = both_contacts(shapes.at[2 * n], n, wait_middle, nothing)
        shapes[2 * n + 1], under[n] = relax([
            (shapes[2 * n], predicted_of[0], touches[0]), (lower[n, 0], predicted_of[1], touches[1])
        ])
        touch = contact(0, shapes.at[2 * n + 1], under.at[n], nothing)
        (shape,) = relax([(shapes[2 * n + 1], predicted_of[0], touch)])
        shapes[2 * n + 2] = shape
    predicted = predicted_of[0]
    send_force(predicted, shape, 0)
    near_copies = [
        remote(shapes.at[ITERS], shapes_near.at[e - 1], near_send.at[e - 1], near_recv.at[e - 1], 0, e)
        for e in range(1, depth + 1)
    ]
    build_ghosts()
    build_deposit()
    build_fluid(0, pop_ref, rim_copies)
    gather_force(0)
    advance(fluid_own)
    lines_own = [
        jnp.concatenate([fluid_own[i, x] for x in range(cx)], axis=0) for i in range(DIRS)
    ]
    density, momentum = moments(lines_own)
    inverse_density = 1.0 / density
    sample([m * inverse_density for m in momentum], 1)
    send_flow(1)
    fill_ring(1, lines_own)
    last_copies = send_sides(1) + send_corners(1)

    for copy in near_copies:
        copy.wait_recv()
    level = [shapes.at[ITERS]] + [shapes_near.at[e - 1] for e in range(1, depth + 1)]
    touches = [contact(e, level[e], level[e + 1], nothing) for e in range(depth)]
    all_bytes(flow_in.at[1], flow_recv.at[1])
    for e in range(depth):
        predicted_of[e] = level[e][...] + time_step * vertex_flow(1, e)
    for sweep in range(ITERS):
        count = ITERS - sweep
        made = relax([(level[e][...], predicted_of[e], touches[e]) for e in range(count)])
        for e in range(count):
            ghosts[sweep, e] = made[e]
        level = [ghosts.at[sweep, e] for e in range(count)]
        touches = [contact(e, level[e], level[e + 1], nothing) for e in range(count - 1)]
    send_force(predicted_of[0], made[0], 1)

    outp_ref[...] = ghosts[ITERS - 1, 0]
    build_fluid(1, fluid_own, last_copies)
    gather_force(1)
    advance(outf_ref)

    for copy in start_copies + middle_copies:
        copy.wait_send()
    for copy in cells_copies + rim_copies + last_copies + ghost_copies + near_copies:
        copy.wait_send()
    for step in range(STEPS):
        all_bytes(flow_out.at[step, pl.ds(0, n_brick - 1)], flow_send.at[step])
        all_bytes(force_in.at[step, pl.ds(0, 3 * n_brick - 1)], force_send.at[step])


def finish_kernel(fluid_ref, rows_ref, outf_ref, outp_ref):
    outf_ref[...] = fluid_ref[...]
    bodies, verts = outp_ref.shape[1:]
    for b in range(bodies):
        for c in range(3):
            r = b * BODY_ROWS + c
            outp_ref[c, b : b + 1, :] = rows_ref[r : r + 1, 0:verts]


def on_device(
    populations, positions, rest_shape, inverse, sample_cells, vertex_slots, pair_own, pair_far
):
    n_brick = lax.axis_size("brick")
    n_group = lax.axis_size("group")
    slot_count = sample_cells.shape[1]
    bodies, verts = positions.shape[1:]
    width = up(verts, LANES)
    rows = bodies * BODY_ROWS
    dirs, cx, cy, lanes = populations.shape
    tiles = pair_own.shape[1] // LANES
    wide = n_brick * GROUP
    long_rows = 3 * cx * (cy + 2 * RING)
    short_rows = (cx + 2) * (cy + 2)
    blocks_v = width // LANES
    edge = verts // LANES * LANES
    main = edge // (2 * LANES) * (2 * LANES)
    f32, bf16, i32 = jnp.float32, jnp.bfloat16, jnp.int32
    vmem = pltpu.VMEM
    dma = pltpu.SemaphoreType.DMA
    in_vmem = pl.BlockSpec(memory_space=pltpu.VMEM)
    fluid, shape_rows = pl.pallas_call(
        functools.partial(step_kernel, (n_brick, n_group, verts, bodies, slot_count)),
        out_shape=(vmem(populations.shape, f32), vmem((rows, width), f32)),
        in_specs=[pl.BlockSpec(memory_space=pltpu.HBM)] * 8,
        out_specs=(in_vmem, in_vmem),
        scratch_shapes=[
            vmem(populations.shape, f32),
            vmem(positions.shape, f32),
            vmem(rest_shape.shape, f32),
            vmem(sample_cells.shape, i32),
            vmem(vertex_slots.shape, i32),
            vmem((2, tiles, LANES), i32),
            vmem((verts, verts), f32),
            vmem((up(max(verts - edge, 1), 8), width), f32),
            vmem((edge, main), bf16),
            vmem((edge, main), bf16),
            vmem((edge, 2 * (edge - main)), bf16),
            vmem((ITERS, 4, tiles, LANES), i32),
            vmem((ITERS, tiles * LANES, LANES), bf16),
            vmem((ITERS, tiles, blocks_v * rows, LANES), bf16),
            vmem((ITERS, 2 * blocks_v * rows, tiles * LANES), bf16),
            vmem((ITERS, rows * tiles, LANES), f32),
            vmem((bodies, width, wide), bf16),
            vmem((3, wide, LANES), bf16),
            vmem((3, 8, wide), i32),
            vmem((ITERS, LANES, LANES), f32),
            vmem((ITERS + 1, rows, width), f32),
            vmem((ITERS // 2, 2, rows, width), f32),
            vmem((ITERS // 2, rows, width), f32),
            vmem((ITERS, rows, width), f32),
            vmem((ITERS - 1, 2, tiles, LANES), i32),
            vmem((ITERS - 1,) + vertex_slots.shape, i32),
            vmem((ITERS, ITERS, rows, width), f32),
            vmem((ITERS, rows, width), f32),
            vmem((rows, width), f32),
            vmem((ITERS, rows, width), i32),
            vmem((ITERS, 1, up(bodies * verts + width, LANES)), i32),
            vmem((1, up(slot_count, LANES)), i32),
            vmem((3, 3, 1, up(slot_count, LANES)), i32),
            vmem((STEPS, n_brick, 1, LANES), f32),
            vmem((STEPS, n_brick, 1, LANES), f32),
            vmem((STEPS, n_brick, 1, LANES), f32),
            vmem((STEPS, 3 * n_brick, 1, LANES), f32),
            vmem((STEPS, 2, 9, cy, LANES), f32),
            vmem((STEPS, 2, 9, cy, LANES), f32),
            vmem((STEPS, 2, 2, 9, 1, LANES), f32),
            vmem((STEPS, 2, 2, 9, 1, LANES), f32),
            vmem((STEPS, 2, dirs, cx, 1, LANES), f32),
            vmem((STEPS, 2, dirs, cx, 1, LANES), f32),
            vmem((dirs, short_rows, LANES), f32),
            vmem((dirs, short_rows, LANES), f32),
            vmem(populations.shape, f32),
            vmem((3, long_rows, LANES), f32),
            vmem((3, short_rows, LANES), f32),
            dma((8,)),
            pltpu.SemaphoreType.REGULAR,
            dma((ITERS // 2, 2)),
            dma((ITERS // 2, 2)),
            dma((ITERS,)),
            dma((ITERS,)),
            dma((ITERS - 1,)),
            dma((ITERS - 1,)),
            dma((ITERS - 1,)),
            dma((ITERS - 1,)),
            dma((STEPS,)),
            dma((STEPS,)),
            dma((STEPS,)),
            dma((STEPS,)),
            dma((8,)),
            dma((8,)),
            dma((STEPS, 2)),
            dma((STEPS, 2)),
            dma((STEPS, 2)),
            dma((STEPS, 2)),
            dma((STEPS, 4)),
            dma((STEPS, 4)),
        ],
        compiler_params=pltpu.CompilerParams(
            collective_id=0, has_side_effects=True, vmem_limit_bytes=48 * 1024 * 1024
        ),
    )(*[
        pltpu.with_memory_space_constraint(value, pltpu.HBM)
        for value in (
            populations, positions, rest_shape, inverse, sample_cells, vertex_slots,
            pair_own.reshape(tiles, LANES), pair_far.reshape(tiles, LANES),
        )
    ])
    return pl.pallas_call(
        finish_kernel,
        out_shape=(
            jax.ShapeDtypeStruct(populations.shape, f32),
            jax.ShapeDtypeStruct(positions.shape, f32),
        ),
        in_specs=[in_vmem, in_vmem],
        out_specs=(in_vmem, in_vmem),
        compiler_params=pltpu.CompilerParams(vmem_limit_bytes=8 * 1024 * 1024),
    )(fluid, shape_rows)


def solution(mesh):
    placed = (
        P(None, "group", "brick", None),
        P(None, ("group", "brick"), None),
        P(),
        P(),
        P(("group", "brick"), None),
        P(("group", "brick"), None),
        P(("group", "brick"), None),
        P(("group", "brick"), None),
    )
    return jax.shard_map(
        on_device,
        mesh=mesh,
        in_specs=placed,
        out_specs=(P(None, "group", "brick", None), P(None, ("group", "brick"), None)),
        check_vma=False,
    )
```

```python
import functools

import jax
import jax.numpy as jnp
from jax import lax
from jax.experimental import pallas as pl
from jax.experimental.pallas import tpu as pltpu
from jax.sharding import PartitionSpec as P

ITERS = 4
STEPS = 2

velocities = [
    (0, 0, 0),
    (0, 0, 1),
    (0, 0, -1),
    (1, 0, 0),
    (-1, 0, 0),
    (0, 1, 0),
    (0, -1, 0),
    (1, 1, 0),
    (-1, -1, 0),
    (1, -1, 0),
    (-1, 1, 0),
    (1, 0, 1),
    (-1, 0, -1),
    (1, 0, -1),
    (-1, 0, 1),
    (0, 1, 1),
    (0, -1, -1),
    (0, 1, -1),
    (0, -1, 1),
]
weights_table = [1.0 / 3.0] + [1.0 / 18.0] * 6 + [1.0 / 36.0] * 12
DIRS = len(velocities)
relax_time = 0.8
contact_gain = 0.5
contact_range = 6.0
coupling_gain = 0.05
mass_weight = 1.0
shape_weight = 1.0
time_step = 1.0

LANES = 128
BODY_ROWS = 4
GROUP = 32
RING = 2
MESH = pl.DeviceIdType.MESH


def up(value, unit):
    return -(-value // unit) * unit


def take(rows, index):
    return jnp.take_along_axis(rows, index, axis=1, mode="promise_in_bounds")


def halves(value):
    high = value.astype(jnp.bfloat16).astype(jnp.float32)
    return high, value - high


def signed_sum(terms, axis):
    total = None
    for p in range(1, DIRS, 2):
        sign = velocities[p][axis]
        if sign == 0:
            continue
        if total is None:
            assert sign > 0
            total = terms[p]
        else:
            total = total + terms[p] if sign > 0 else total - terms[p]
    return total


def moments(rows):
    density = functools.reduce(lambda a, b: a + b, rows)
    opposite = {p: rows[p] - rows[p + 1] for p in range(1, DIRS, 2)}
    return density, [signed_sum(opposite, axis) for axis in range(3)]


def dot_c(vector, p):
    total = None
    for axis in range(3):
        sign = velocities[p][axis]
        if sign == 0:
            continue
        if total is None:
            total = vector[axis] if sign > 0 else -vector[axis]
        else:
            total = total + vector[axis] if sign > 0 else total - vector[axis]
    return total


def collide(rows, force):
    density, momentum = moments(rows)
    inverse_density = 1.0 / density
    veloc = [(momentum[a] + 0.5 * force[a]) * inverse_density for a in range(3)]
    square = veloc[0] * veloc[0] + veloc[1] * veloc[1] + veloc[2] * veloc[2]
    keep, gain = 1.0 - 1.0 / relax_time, 1.0 / relax_time
    base = 1.0 - 1.5 * square
    scaled = [density * (gain * w) for w in (1.0 / 3.0, 1.0 / 18.0, 1.0 / 36.0)]
    out = [None] * DIRS
    out[0] = keep * rows[0] + scaled[0] * base
    for p in range(1, DIRS, 2):
        weight = weights_table[p]
        rho = scaled[1] if p < 7 else scaled[2]
        along = dot_c(veloc, p)
        even = rho * (base + 4.5 * (along * along))
        odd = rho * (3.0 * along) + (3.0 * weight) * dot_c(force, p)
        out[p] = keep * rows[p] + (even + odd)
        out[p + 1] = keep * rows[p + 1] + (even - odd)
    return out


def far_dirs(sign):
    known = [i for i in range(DIRS) if velocities[i][0] == sign]
    return known + [velocities.index((-sign, 0, 0)), velocities.index((0, 1, 0)), velocities.index((0, 0, 1)), 0]


def far_rows(rows, sign):
    density, momentum = moments(rows)
    known = far_dirs(sign)[:5]
    ahead = functools.reduce(lambda a, b: a + b, [rows[i] for i in known])
    back = ahead - momentum[0] if sign > 0 else ahead + momentum[0]
    at = velocities.index
    side = momentum[1] - (rows[at((sign, 1, 0))] - rows[at((sign, -1, 0))])
    along = momentum[2] - (rows[at((sign, 0, 1))] - rows[at((sign, 0, -1))])
    return [rows[i] for i in known] + [back, side, along, density - ahead - back - side - along]


def roll_z(value, index):
    step = velocities[index][2]
    if step == 0:
        return value
    return pltpu.roll(value, step % LANES, 1)


def step_kernel(
    sizes, pop_hbm, pos_hbm, rest_hbm, inv_hbm, cells_hbm, slots_hbm, own_hbm, far_hbm,
    outf_ref, outp_ref,
    pop_ref, pos_ref, rest_in, cells_ref, slots_ref, pairs,
    inv_raw, inv_tail, inv_high, inv_mid, inv_last, places, hot, mask, lhs, spread, slot_hot, deposit, row_id, turned,
    shapes, lower, under, shapes_near, pairs_near, slots_near, ghosts, predicted_of,
    rest8, slot8, slot_flat, cells_own, cells_near,
    flow_out, flow_in, force_out, force_in, far_out, far_in, corner_out, corner_in, edges_out, edges_in, fluid, post, fluid_own,
    field, field_near,
    in_sem, ready, ring_send, ring_recv, near_send, near_recv, pairs_send, pairs_recv, slots_send, slots_recv, flow_send, flow_recv, force_send, force_recv,
    cells_send, cells_recv, edge_send, edge_recv, far_send, far_recv, corner_send, corner_recv,
):
    n_brick, n_group, verts, bodies, slot_count = sizes
    me = lax.axis_index("brick")
    group = lax.axis_index("group")
    cx, cy = pop_ref.shape[1:3]
    width = shapes.shape[2]
    blocks_v = width // LANES
    rows_v = bodies * BODY_ROWS
    tiles = pairs.shape[1]
    depth = ITERS
    peer_cells = slot_count // n_brick
    wide = n_brick * GROUP
    wide_tiles = wide // LANES
    slot_tiles = cells_own.shape[1] // LANES
    long_y = cy + 2 * RING
    short_y = cy + 2
    part = cx * long_y
    f32, bf16, i32 = jnp.float32, jnp.bfloat16, jnp.int32

    def brick_at(offset):
        return lax.rem(me + (offset + n_brick), n_brick)

    def group_at(offset):
        return lax.rem(group + (offset + n_group), n_group)

    def iota(shape, axis):
        return lax.broadcasted_iota(i32, shape, axis)

    by_reach = sorted(range(n_brick), key=lambda o: -min(o, n_brick - o))
    near = [(dg, o) for dg in (1, -1, 0) for o in by_reach if (dg, o) != (0, 0)]
    first = [(0, o) for o in range(1, n_brick)] + [(1, 0), (-1, 0)]
    barrier = pltpu.get_barrier_semaphore()
    for dg, o in first:
        pl.semaphore_signal(barrier, inc=1, device_id=(group_at(dg), brick_at(o)), device_id_type=MESH)
    loads = [
        pltpu.make_async_copy(source, target, in_sem.at[n])
        for n, (source, target) in enumerate([
            (pop_hbm, pop_ref), (cells_hbm, cells_ref), (pos_hbm, pos_ref), (rest_hbm, rest_in),
            (own_hbm, pairs.at[0]), (far_hbm, pairs.at[1]), (slots_hbm, slots_ref), (inv_hbm, inv_raw),
        ])
    ]
    for load in loads:
        load.start()
    inv_copy = loads.pop()
    for load in loads:
        load.wait()

    def remote(source, target, send, recv, dg, o):
        copy = pltpu.make_async_remote_copy(
            src_ref=source, dst_ref=target, send_sem=send, recv_sem=recv,
            device_id=(group_at(dg), brick_at(o)), device_id_type=MESH,
        )
        copy.start()
        return copy

    def all_bytes(ref, sem):
        pltpu.make_async_copy(ref, ref, sem).wait()

    shapes[0] = jnp.zeros((rows_v, width), f32)
    rest8[...] = jnp.zeros((rows_v, width), f32)
    for b in range(bodies):
        for c in range(3):
            r = b * BODY_ROWS + c
            shapes[0, r : r + 1, 0:verts] = pos_ref[c, b : b + 1, :]
            rest8[r : r + 1, 0:verts] = rest_in[c : c + 1, :]
    cells_own[...] = jnp.zeros(cells_own.shape, i32)
    cells_own[:, 0:slot_count] = cells_ref[...]
    lane8 = iota((8, LANES), 1)
    sub8 = iota((8, LANES), 0)
    in_group = lane8 % GROUP
    of_group = lane8 // GROUP

    def sample(flow, step):
        lines = cx * cy
        got = []
        for t in range(slot_tiles):
            cell = cells_own[0:1, t * LANES : (t + 1) * LANES]
            at = jnp.broadcast_to(cell & (LANES - 1), (lines, LANES))
            chosen = jnp.broadcast_to(cell >> 7, (lines, LANES)) == iota((lines, LANES), 0)
            got.append([
                jnp.sum(jnp.where(chosen, take(flow[c], at), 0.0), axis=0, keepdims=True) for c in range(3)
            ])
        for base in range(0, n_brick, 8):
            owner = base + sub8 - in_group // peer_cells
            owner = jnp.where(owner < 0, owner + n_brick, owner)
            slot = owner * peer_cells + in_group % peer_cells
            touched = {(base + n) % n_brick * peer_cells // LANES for n in range(1 - depth, 8)}
            message = jnp.zeros((8, LANES), f32)
            for c in range(3):
                for t in sorted(touched):
                    moved = take(jnp.broadcast_to(got[t][c], (8, LANES)), slot & (LANES - 1))
                    message = jnp.where((of_group == c) & (slot >> 7 == t), moved, message)
            for s in range(8):
                flow_out[step, base + s] = message[s : s + 1, :]

    def send_flow(step):
        pltpu.make_async_copy(flow_out.at[step, me], flow_in.at[step, me], flow_recv.at[step]).start()
        for o in by_reach[:-1]:
            remote(
                flow_out.at[step, brick_at(o)], flow_in.at[step, me],
                flow_send.at[step], flow_recv.at[step], 0, o,
            )

    def send_shapes(n):
        return [
            remote(
                shapes.at[2 * n], lower.at[n, e - 1], ring_send.at[n, e - 1], ring_recv.at[n, e - 1], 0, e
            )
            for e in ((2, 1) if n else (1, 2))
        ]

    def send_pairs(e):
        return remote(pairs, pairs_near.at[e - 1], pairs_send.at[e - 1], pairs_recv.at[e - 1], 0, e)

    def send_slots(e):
        return remote(slots_ref, slots_near.at[e - 1], slots_send.at[e - 1], slots_recv.at[e - 1], 0, e)

    lines_own = [
        jnp.concatenate([pop_ref[i, x] for x in range(cx)], axis=0) for i in range(DIRS)
    ]
    density, momentum = moments(lines_own)
    inverse_density = 1.0 / density
    sample([m * inverse_density for m in momentum], 0)

    pl.semaphore_wait(barrier, len(first))
    for dg in (1, -1):
        pl.semaphore_signal(ready, inc=1, device_id=(group_at(dg), brick_at(0)), device_id_type=MESH)
    send_flow(0)
    start_copies = send_shapes(0)
    ghost_copies = [send_pairs(1), send_slots(1)]
    def fill_ring(step, lines):
        for n, sign in enumerate((1, -1)):
            close = cx - 1 if sign > 0 else 0
            for m, value in enumerate(far_rows(lines, sign)):
                far_out[step, n, m] = value[close * cy : (close + 1) * cy]
                for side, y in enumerate((0, cy - 1)):
                    corner_out[step, n, side, m] = value[close * cy + y : close * cy + y + 1]
        for i in range(DIRS):
            for x in range(cx):
                for side, y in enumerate((0, cy - 1)):
                    edges_out[step, side, i, x] = lines[i][x * cy + y : x * cy + y + 1]

    def send_sides(step):
        return [
            remote(
                far_out.at[step, n], far_in.at[step, n], far_send.at[step, n], far_recv.at[step, n], dg, 0
            )
            for n, dg in enumerate((1, -1))
        ] + [
            remote(
                edges_out.at[step, side], edges_in.at[step, side],
                edge_send.at[step, side], edge_recv.at[step, side], 0, 2 * side - 1,
            )
            for side in (0, 1)
        ]

    def send_corners(step):
        return [
            remote(
                corner_out.at[step, n, side], corner_in.at[step, n, side],
                corner_send.at[step, 2 * n + side], corner_recv.at[step, 2 * n + side], dg, 2 * side - 1,
            )
            for n, dg in enumerate((1, -1))
            for side in (0, 1)
        ]

    lines_own = [
        jnp.concatenate([pop_ref[i, x] for x in range(cx)], axis=0) for i in range(DIRS)
    ]
    fill_ring(0, lines_own)
    rim_copies = send_sides(0)

    def place(index):
        body = jnp.zeros(index.shape, i32)
        for b in range(1, bodies):
            body = body + jnp.where(index >= b * verts, 1, 0)
        vertex = index - body * verts
        return vertex & (LANES - 1), vertex >> 7, body

    lane_square = iota((LANES, LANES), 1)

    def build_pairs(e, ref):
        own_lane, own_block, own_body = place(ref[0])
        far_lane, far_block, far_body = place(ref[1])
        places[e, 0] = own_lane
        places[e, 1] = own_body * blocks_v + own_block
        places[e, 2] = far_lane
        places[e, 3] = far_body * blocks_v + far_block
        turned[e, 0:tiles, :] = own_lane.astype(f32)
        turned[e, tiles:LANES, :] = jnp.zeros((LANES - tiles, LANES), f32)
        columns = jnp.transpose(turned[e]).astype(i32)
        for t in range(tiles):
            column = jnp.broadcast_to(columns[:, t : t + 1], (LANES, LANES))
            hot[e, t * LANES : (t + 1) * LANES, :] = jnp.where(column == lane_square, 1.0, 0.0).astype(bf16)
            chosen = jnp.broadcast_to(own_block[t : t + 1, :], (blocks_v * rows_v, LANES))
            mask[e, t] = jnp.where(
                chosen == iota((blocks_v * rows_v, LANES), 0) // rows_v, 1.0, 0.0
            ).astype(bf16)

    def place_slots(e, ref):
        slot_flat[e, :, 0 : bodies * verts] = ref[...]
        total = slot_flat.shape[2]
        flat = jnp.broadcast_to(slot_flat[e], (8, total))
        picked = flat[:, :width]
        row_body = iota((rows_v, width), 0) // BODY_ROWS
        for b in range(1, bodies):
            moved = pltpu.roll(flat, total - b * verts, 1)[:, :width]
            picked = jnp.where(row_body == b, moved, picked)
        slot8[e] = jnp.where(iota((rows_v, width), 1) < verts, picked, -1)

    slot_flat[...] = jnp.zeros(slot_flat.shape, i32)
    spread[...] = jnp.zeros(spread.shape, f32)
    build_pairs(0, pairs)
    place_slots(0, slots_ref)

    def build_ghosts():
        for copy in ghost_copies[2:]:
            copy.wait_recv()
        for e in range(2, depth):
            build_pairs(e, pairs_near.at[e - 1])
            place_slots(e, slots_near.at[e - 1])

    inv_copy.wait()
    chunk = 32
    edge = verts // LANES * LANES
    tail = verts - edge
    main = inv_high.shape[1]
    inv_tail[...] = jnp.zeros(inv_tail.shape, f32)
    inv_tail[0:tail, 0:verts] = inv_raw[edge:verts, :]

    def split(n, _):
        at = pl.multiple_of(n * chunk, chunk)
        high, mid = halves(inv_raw[pl.ds(at, chunk), 0:edge])
        high = high.astype(bf16)
        mid = mid.astype(bf16)
        inv_high[pl.ds(at, chunk), :] = high[:, :main]
        inv_mid[pl.ds(at, chunk), :] = mid[:, :main]
        inv_last[pl.ds(at, chunk), 0 : edge - main] = high[:, main:]
        inv_last[pl.ds(at, chunk), edge - main : 2 * (edge - main)] = mid[:, main:]
        return 0

    lax.fori_loop(0, edge // chunk, split, 0)

    def pick(ref, lane, ident):
        total = [jnp.zeros((tiles, LANES), f32)] * 3
        for b in range(bodies):
            for h in range(blocks_v):
                chosen = ident == b * blocks_v + h
                for c in range(3):
                    r = b * BODY_ROWS + c
                    row = ref[r : r + 1, h * LANES : (h + 1) * LANES]
                    got = take(jnp.broadcast_to(row, (tiles, LANES)), lane)
                    total[c] = jnp.where(chosen, got, total[c])
        return total

    def contact(e, shape_of, lower_of, before_far):
        own_id = places[e, 1]
        own = pick(shape_of, places[e, 0], own_id)
        before_far()
        far = pick(lower_of, places[e, 2], places[e, 3])
        diff = [a - b for a, b in zip(own, far)]
        square = diff[0] * diff[0] + diff[1] * diff[1] + diff[2] * diff[2]
        scale = contact_gain * jnp.exp(-square / contact_range)
        for b in range(bodies):
            inside = (own_id >= b * blocks_v) & (own_id < (b + 1) * blocks_v)
            for c in range(3):
                r = b * BODY_ROWS + c
                spread[e, r * tiles : (r + 1) * tiles, :] = jnp.where(inside, scale * diff[c], 0.0)
        half = blocks_v * rows_v
        for t in range(tiles):
            push = spread[e, pl.ds(t, rows_v, stride=tiles), :]
            for n, piece in enumerate(halves(push)):
                pair = jnp.concatenate([piece, piece], axis=0).astype(bf16)
                lhs[e, n * half : (n + 1) * half, t * LANES : (t + 1) * LANES] = (
                    jnp.concatenate([pair] * (blocks_v // 2), axis=0) * mask[e, t]
                )
        middle = tiles // 2 * LANES
        added = jnp.dot(lhs[e, :, :middle], hot[e, :middle], preferred_element_type=f32)
        added = added + jnp.dot(lhs[e, :, middle:], hot[e, middle:], preferred_element_type=f32)
        added = added[:half] + added[half:]
        return jnp.concatenate([added[h * rows_v : (h + 1) * rows_v] for h in range(blocks_v)], axis=1)

    def received(step, e):
        out = []
        per_tile = LANES // peer_cells
        for t in range(slot_tiles):
            index = (sub8 % BODY_ROWS) * GROUP + e * peer_cells + lane8 % peer_cells
            table = jnp.zeros((8, LANES), f32)
            for s in range(t * per_tile, min((t + 1) * per_tile, n_brick)):
                moved = take(jnp.broadcast_to(flow_in[step, s], (8, LANES)), index)
                table = jnp.where(lane8 // peer_cells == s % per_tile, moved, table)
            out.append(table)
        return out

    def vertex_flow(step, e):
        tables = received(step, e)
        parts = []
        for h in range(blocks_v):
            slot = jnp.maximum(slot8[e, :, h * LANES : (h + 1) * LANES], 0)
            got = take(tables[0], slot & (LANES - 1))
            for t in range(1, slot_tiles):
                got = jnp.where(slot >> 7 == t, take(tables[t], slot & (LANES - 1)), got)
            parts.append(got)
        return jnp.concatenate(parts, axis=1)

    def relax(cases):
        high, mid, ends = [], [], []
        for shape, predicted, touch in cases:
            centroid = jnp.sum(shape, axis=1, keepdims=True) * (1.0 / verts)
            rhs = mass_weight * predicted + shape_weight * (centroid + rest8[...]) + touch
            a, b = halves(rhs[:, :edge])
            high.append(a)
            mid.append(b)
            more = jnp.zeros((rows_v, edge), f32)
            last = jnp.zeros((rows_v, LANES), f32)
            for n in range(tail):
                row = inv_tail[n : n + 1, :]
                more = more + rhs[:, edge + n : edge + n + 1] * row[:, :edge]
                value = jnp.sum(rhs * row, axis=1, keepdims=True)
                last = jnp.where(iota((rows_v, LANES), 1) == n, value, last)
            ends.append((more, last))
        if len(cases) % 2:
            high.append(jnp.zeros((rows_v, edge), f32))
            mid.append(jnp.zeros((rows_v, edge), f32))
        count = len(high) * rows_v
        high = jnp.concatenate(high, axis=0).astype(bf16)
        left = jnp.concatenate([high, jnp.concatenate(mid, axis=0).astype(bf16)], axis=0)
        both = jnp.dot(left, inv_high[...], preferred_element_type=f32)
        rest = jnp.dot(high, inv_mid[...], preferred_element_type=f32)
        final = jnp.dot(left, inv_last[...], preferred_element_type=f32)
        both = both[:count] + both[count:] + rest
        step = edge - main
        final = final[:count, :step] + final[count:, :step] + final[:count, step:]
        out = []
        for n, (more, last) in enumerate(ends):
            rows = slice(n * rows_v, (n + 1) * rows_v)
            out.append(jnp.concatenate(
                [both[rows] + more[:, :main], final[rows] + more[:, main:], last], axis=1
            ))
        return out

    def build_slots():
        column_of = []
        for h in range(blocks_v):
            rows = slot8[0, :, h * LANES : (h + 1) * LANES].astype(f32)
            turned[0, h * rows_v : (h + 1) * rows_v, :] = rows
        columns = jnp.transpose(turned[0]).astype(i32)
        for t in range(wide_tiles):
            q = iota((LANES, LANES), 1)
            brick = q // GROUP + t * (LANES // GROUP)
            inner = q % GROUP
            target = brick - 1 + inner // peer_cells
            target = jnp.where(target < 0, target + n_brick, target)
            target = jnp.where(target >= n_brick, target - n_brick, target)
            slot = jnp.where(inner < 3 * peer_cells, target * peer_cells + inner % peer_cells, -2)
            for b in range(bodies):
                for h in range(blocks_v):
                    at = h * rows_v + b * BODY_ROWS
                    column = jnp.broadcast_to(columns[:, at : at + 1], (LANES, LANES))
                    slot_hot[b, h * LANES : (h + 1) * LANES, t * LANES : (t + 1) * LANES] = jnp.where(
                        column == slot, 1.0, 0.0
                    ).astype(bf16)

    def build_deposit():
        for copy in cells_copies:
            copy.wait_recv()
        per_tile = LANES // GROUP
        for dg in range(3):
            for t in range(wide_tiles):
                start = t * per_tile * peer_cells
                source, offset = start // LANES, start % LANES
                index = offset + of_group * peer_cells + in_group % peer_cells
                side = in_group // peer_cells
                cell = jnp.zeros((8, LANES), i32)
                for db in range(3):
                    ref = cells_own if (dg, db) == (1, 1) else cells_near.at[dg, db]
                    row = ref[0:1, source * LANES : (source + 1) * LANES]
                    moved = take(jnp.broadcast_to(row, (8, LANES)), index)
                    cell = jnp.where(side == db, moved, cell)
                line = cell >> 7
                x = jnp.zeros((8, LANES), i32)
                for edge_x in range(1, cx):
                    x = x + jnp.where(line >= edge_x * cy, 1, 0)
                y = line - x * cy + cy * (side - 1) + RING
                inside = (y >= 0) & (y < long_y) & (side < 3)
                at = dg * wide_tiles + t
                row_id[dg, :, t * LANES : (t + 1) * LANES] = jnp.where(inside, x * long_y + y, -1)
                turned[1, at : at + 1, :] = (cell & (LANES - 1))[0:1, :].astype(f32)
        columns = jnp.transpose(turned[1]).astype(i32)
        for dg in range(3):
            for t in range(wide_tiles):
                at = dg * wide_tiles + t
                column = jnp.broadcast_to(columns[:, at : at + 1], (LANES, LANES))
                deposit[dg, t * LANES : (t + 1) * LANES, :] = jnp.where(
                    column == lane_square, 1.0, 0.0
                ).astype(bf16)

    def build_fluid(step, own, copies):
        for copy in copies:
            copy.wait_recv()

        def put(i, plane, middle, lower_end, upper_end):
            at = plane * short_y
            fluid[i, at + 1 : at + 1 + cy, :] = middle
            fluid[i, at : at + 1, :] = lower_end
            fluid[i, at + 1 + cy : at + short_y, :] = upper_end

        for i in range(DIRS):
            for x in range(cx):
                put(i, x + 1, own[i, x], edges_in[step, 1, i, x], edges_in[step, 0, i, x])
            for n, (plane, sign) in enumerate(((0, 1), (cx + 1, -1))):
                kept = far_dirs(sign)
                if i in kept:
                    m = kept.index(i)
                    put(i, plane, far_in[step, n, m], corner_in[step, n, 1, m], corner_in[step, n, 0, m])
                else:
                    fluid[i, plane * short_y : (plane + 1) * short_y, :] = jnp.zeros((short_y, LANES), f32)

    def advance(target):
        for c in range(3):
            for x in range(cx + 2):
                at = (x + 1) * long_y + 1
                field_near[c, x * short_y : (x + 1) * short_y, :] = field[c, at : at + short_y, :]
        for q in range((cx + 2) * short_y // 8):
            rows = slice(8 * q, 8 * q + 8)
            after = collide(
                [fluid[i, rows, :] for i in range(DIRS)], [field_near[c, rows, :] for c in range(3)]
            )
            for i in range(DIRS):
                post[i, rows, :] = roll_z(after[i], i)
        for i in range(DIRS):
            step_x, step_y, _ = velocities[i]
            for x in range(cx):
                at = (x + 1 - step_x) * short_y + 1 - step_y
                target[i, x] = post[i, at : at + cy, :]

    def send_force(predicted, shape, step):
        change = coupling_gain * (shape - predicted)
        left = jnp.concatenate(halves(change), axis=0).astype(bf16)
        total = None
        for b in range(bodies):
            got = jnp.dot(left, slot_hot[b], preferred_element_type=f32)
            got = got[:rows_v] + got[rows_v:]
            if b:
                got = pltpu.roll(got, rows_v - b * BODY_ROWS, 0)
            total = got if total is None else total + got
        per_tile = LANES // GROUP
        index = (sub8 % per_tile) * GROUP + in_group
        for base in range(0, n_brick, 8):
            message = jnp.zeros((8, LANES), f32)
            for c in range(3):
                for n in range(8 // per_tile):
                    t = base // per_tile + n
                    row = total[c : c + 1, t * LANES : (t + 1) * LANES]
                    moved = take(jnp.broadcast_to(row, (8, LANES)), index)
                    chosen = (of_group == c) & (sub8 // per_tile == n)
                    message = jnp.where(chosen, moved, message)
            for s in range(8):
                force_out[step, base + s] = message[s : s + 1, :]
        pltpu.make_async_copy(
            force_out.at[step, me], force_in.at[step, n_brick + me], force_recv.at[step]
        ).start()
        for dg, o in near:
            remote(
                force_out.at[step, brick_at(o)], force_in.at[step, (1 - dg) * n_brick + me],
                force_send.at[step], force_recv.at[step], dg, o,
            )

    def gather_force(step):
        all_bytes(force_in.at[step], force_recv.at[step])
        per_tile = LANES // GROUP
        index = jnp.minimum(sub8, 3) * GROUP + in_group
        for dg in range(3):
            parts = []
            for t in range(wide_tiles):
                table = jnp.zeros((8, LANES), f32)
                for n in range(per_tile):
                    row = force_in[step, dg * n_brick + t * per_tile + n]
                    moved = take(jnp.broadcast_to(row, (8, LANES)), index)
                    table = jnp.where(of_group == n, moved, table)
                parts.append(table)
            table = jnp.concatenate(parts, axis=1)
            ids = jnp.broadcast_to(row_id[dg, 0:1, :], (part, wide))
            chosen = ids == iota((part, wide), 0)
            left = []
            pieces = halves(table)
            for c in range(3):
                for piece in pieces:
                    row = jnp.broadcast_to(piece[c : c + 1, :], (part, wide))
                    left.append(jnp.where(chosen, row, 0.0))
            left = jnp.concatenate(left, axis=0).astype(bf16)
            got = jnp.dot(left, deposit[dg], preferred_element_type=f32)
            for c in range(3):
                field[c, dg * part : (dg + 1) * part, :] = (
                    got[2 * c * part : (2 * c + 1) * part] + got[(2 * c + 1) * part : (2 * c + 2) * part]
                )

    def nothing():
        pass

    def both_contacts(own, n, before_far, between):
        first_touch = contact(0, own, lower.at[n, 0], before_far)
        between()
        return [first_touch, contact(1, lower.at[n, 0], lower.at[n, 1], nothing)]

    def wait_start():
        start_copies[0].wait_recv()

    def wait_under():
        for copy in ghost_copies[:2]:
            copy.wait_recv()
        build_pairs(1, pairs_near.at[0])
        place_slots(1, slots_near.at[0])
        start_copies[1].wait_recv()

    def wait_middle():
        build_slots()
        for copy in middle_copies:
            copy.wait_recv()

    touches = both_contacts(shapes.at[0], 0, wait_start, wait_under)
    pl.semaphore_wait(ready, 2)
    cells_copies = []
    for n, (dg, db) in enumerate([(a, b) for a in (-1, 0, 1) for b in (-1, 0, 1) if (a, b) != (0, 0)]):
        cells_copies.append(remote(
            cells_own, cells_near.at[1 - dg, 1 - db], cells_send.at[n], cells_recv.at[n], dg, db
        ))
    rim_copies += send_corners(0)
    for e in range(2, depth):
        ghost_copies += [send_pairs(e), send_slots(e)]
    all_bytes(flow_in.at[0], flow_recv.at[0])
    predicted_of[0] = shapes[0] + time_step * vertex_flow(0, 0)
    predicted_of[1] = lower[0, 0] + time_step * vertex_flow(0, 1)
    for n in range(ITERS // 2):
        if n:
            middle_copies = send_shapes(n)
            touches = both_contacts(shapes.at[2 * n], n, wait_middle, nothing)
        shapes[2 * n + 1], under[n] = relax([
            (shapes[2 * n], predicted_of[0], touches[0]), (lower[n, 0], predicted_of[1], touches[1])
        ])
        touch = contact(0, shapes.at[2 * n + 1], under.at[n], nothing)
        (shape,) = relax([(shapes[2 * n + 1], predicted_of[0], touch)])
        shapes[2 * n + 2] = shape
    predicted = predicted_of[0]
    send_force(predicted, shape, 0)
    near_copies = [
        remote(shapes.at[ITERS], shapes_near.at[e - 1], near_send.at[e - 1], near_recv.at[e - 1], 0, e)
        for e in range(1, depth + 1)
    ]
    build_ghosts()
    build_deposit()
    build_fluid(0, pop_ref, rim_copies)
    gather_force(0)
    advance(fluid_own)
    lines_own = [
        jnp.concatenate([fluid_own[i, x] for x in range(cx)], axis=0) for i in range(DIRS)
    ]
    density, momentum = moments(lines_own)
    inverse_density = 1.0 / density
    sample([m * inverse_density for m in momentum], 1)
    send_flow(1)
    fill_ring(1, lines_own)
    last_copies = send_sides(1) + send_corners(1)

    for copy in near_copies:
        copy.wait_recv()
    level = [shapes.at[ITERS]] + [shapes_near.at[e - 1] for e in range(1, depth + 1)]
    touches = [contact(e, level[e], level[e + 1], nothing) for e in range(depth)]
    all_bytes(flow_in.at[1], flow_recv.at[1])
    for e in range(depth):
        predicted_of[e] = level[e][...] + time_step * vertex_flow(1, e)
    for sweep in range(ITERS):
        count = ITERS - sweep
        made = relax([(level[e][...], predicted_of[e], touches[e]) for e in range(count)])
        for e in range(count):
            ghosts[sweep, e] = made[e]
        level = [ghosts.at[sweep, e] for e in range(count)]
        touches = [contact(e, level[e], level[e + 1], nothing) for e in range(count - 1)]
    send_force(predicted_of[0], made[0], 1)

    outp_ref[...] = ghosts[ITERS - 1, 0]
    build_fluid(1, fluid_own, last_copies)
    gather_force(1)
    advance(outf_ref)

    for copy in start_copies + middle_copies:
        copy.wait_send()
    for copy in cells_copies + rim_copies + last_copies + ghost_copies + near_copies:
        copy.wait_send()
    for step in range(STEPS):
        all_bytes(flow_out.at[step, pl.ds(0, n_brick - 1)], flow_send.at[step])
        all_bytes(force_in.at[step, pl.ds(0, 3 * n_brick - 1)], force_send.at[step])


def finish_kernel(fluid_ref, rows_ref, outf_ref, outp_ref):
    outf_ref[...] = fluid_ref[...]
    bodies, verts = outp_ref.shape[1:]
    for b in range(bodies):
        for c in range(3):
            r = b * BODY_ROWS + c
            outp_ref[c, b : b + 1, :] = rows_ref[r : r + 1, 0:verts]


def on_device(
    populations, positions, rest_shape, inverse, sample_cells, vertex_slots, pair_own, pair_far
):
    n_brick = lax.axis_size("brick")
    n_group = lax.axis_size("group")
    slot_count = sample_cells.shape[1]
    bodies, verts = positions.shape[1:]
    width = up(verts, LANES)
    rows = bodies * BODY_ROWS
    dirs, cx, cy, lanes = populations.shape
    tiles = pair_own.shape[1] // LANES
    wide = n_brick * GROUP
    long_rows = 3 * cx * (cy + 2 * RING)
    short_rows = (cx + 2) * (cy + 2)
    blocks_v = width // LANES
    edge = verts // LANES * LANES
    main = edge // (2 * LANES) * (2 * LANES)
    f32, bf16, i32 = jnp.float32, jnp.bfloat16, jnp.int32
    vmem = pltpu.VMEM
    dma = pltpu.SemaphoreType.DMA
    in_vmem = pl.BlockSpec(memory_space=pltpu.VMEM)
    fluid, shape_rows = pl.pallas_call(
        functools.partial(step_kernel, (n_brick, n_group, verts, bodies, slot_count)),
        out_shape=(vmem(populations.shape, f32), vmem((rows, width), f32)),
        in_specs=[pl.BlockSpec(memory_space=pltpu.HBM)] * 8,
        out_specs=(in_vmem, in_vmem),
        scratch_shapes=[
            vmem(populations.shape, f32),
            vmem(positions.shape, f32),
            vmem(rest_shape.shape, f32),
            vmem(sample_cells.shape, i32),
            vmem(vertex_slots.shape, i32),
            vmem((2, tiles, LANES), i32),
            vmem((verts, verts), f32),
            vmem((up(max(verts - edge, 1), 8), width), f32),
            vmem((edge, main), bf16),
            vmem((edge, main), bf16),
            vmem((edge, 2 * (edge - main)), bf16),
            vmem((ITERS, 4, tiles, LANES), i32),
            vmem((ITERS, tiles * LANES, LANES), bf16),
            vmem((ITERS, tiles, blocks_v * rows, LANES), bf16),
            vmem((ITERS, 2 * blocks_v * rows, tiles * LANES), bf16),
            vmem((ITERS, rows * tiles, LANES), f32),
            vmem((bodies, width, wide), bf16),
            vmem((3, wide, LANES), bf16),
            vmem((3, 8, wide), i32),
            vmem((ITERS, LANES, LANES), f32),
            vmem((ITERS + 1, rows, width), f32),
            vmem((ITERS // 2, 2, rows, width), f32),
            vmem((ITERS // 2, rows, width), f32),
            vmem((ITERS, rows, width), f32),
            vmem((ITERS - 1, 2, tiles, LANES), i32),
            vmem((ITERS - 1,) + vertex_slots.shape, i32),
            vmem((ITERS, ITERS, rows, width), f32),
            vmem((ITERS, rows, width), f32),
            vmem((rows, width), f32),
            vmem((ITERS, rows, width), i32),
            vmem((ITERS, 1, up(bodies * verts + width, LANES)), i32),
            vmem((1, up(slot_count, LANES)), i32),
            vmem((3, 3, 1, up(slot_count, LANES)), i32),
            vmem((STEPS, n_brick, 1, LANES), f32),
            vmem((STEPS, n_brick, 1, LANES), f32),
            vmem((STEPS, n_brick, 1, LANES), f32),
            vmem((STEPS, 3 * n_brick, 1, LANES), f32),
            vmem((STEPS, 2, 9, cy, LANES), f32),
            vmem((STEPS, 2, 9, cy, LANES), f32),
            vmem((STEPS, 2, 2, 9, 1, LANES), f32),
            vmem((STEPS, 2, 2, 9, 1, LANES), f32),
            vmem((STEPS, 2, dirs, cx, 1, LANES), f32),
            vmem((STEPS, 2, dirs, cx, 1, LANES), f32),
            vmem((dirs, short_rows, LANES), f32),
            vmem((dirs, short_rows, LANES), f32),
            vmem(populations.shape, f32),
            vmem((3, long_rows, LANES), f32),
            vmem((3, short_rows, LANES), f32),
            dma((8,)),
            pltpu.SemaphoreType.REGULAR,
            dma((ITERS // 2, 2)),
            dma((ITERS // 2, 2)),
            dma((ITERS,)),
            dma((ITERS,)),
            dma((ITERS - 1,)),
            dma((ITERS - 1,)),
            dma((ITERS - 1,)),
            dma((ITERS - 1,)),
            dma((STEPS,)),
            dma((STEPS,)),
            dma((STEPS,)),
            dma((STEPS,)),
            dma((8,)),
            dma((8,)),
            dma((STEPS, 2)),
            dma((STEPS, 2)),
            dma((STEPS, 2)),
            dma((STEPS, 2)),
            dma((STEPS, 4)),
            dma((STEPS, 4)),
        ],
        compiler_params=pltpu.CompilerParams(
            collective_id=0, has_side_effects=True, vmem_limit_bytes=48 * 1024 * 1024
        ),
    )(*[
        pltpu.with_memory_space_constraint(value, pltpu.HBM)
        for value in (
            populations, positions, rest_shape, inverse, sample_cells, vertex_slots,
            pair_own.reshape(tiles, LANES), pair_far.reshape(tiles, LANES),
        )
    ])
    return pl.pallas_call(
        finish_kernel,
        out_shape=(
            jax.ShapeDtypeStruct(populations.shape, f32),
            jax.ShapeDtypeStruct(positions.shape, f32),
        ),
        in_specs=[in_vmem, in_vmem],
        out_specs=(in_vmem, in_vmem),
        compiler_params=pltpu.CompilerParams(vmem_limit_bytes=8 * 1024 * 1024),
    )(fluid, shape_rows)


def solution(mesh):
    placed = (
        P(None, "group", "brick", None),
        P(None, ("group", "brick"), None),
        P(),
        P(),
        P(("group", "brick"), None),
        P(("group", "brick"), None),
        P(("group", "brick"), None),
        P(("group", "brick"), None),
    )
    return jax.shard_map(
        on_device,
        mesh=mesh,
        in_specs=placed,
        out_specs=(P(None, "group", "brick", None), P(None, ("group", "brick"), None)),
        check_vma=False,
    )
```
